256 devices in a mesh: rows: 64 (over z_hi, y, x, core), ch: 4 (over z_lo).
Axes of the slice: x: 4, y: 4, z: 8 (z_hi: 2, z_lo: 4; z = z_hi * 4 + z_lo), core: 2. Of those that a mesh axis runs over, the one named last changes fastest.
Arguments:
- pixels: bfloat16 [256, 96, 2048], P('rows', 'ch'), may hold values from -6 to 6
- depth_weight: float32 [96, 9], P('ch'), may hold values from -2 to 2
- mix_weight: bfloat16 [96, 96], replicated, may hold values from -0.625 to 0.625
- spectral_real: bfloat16 [256, 96, 1024], P(None, 'ch', 'rows'), may hold values from -4 to 4
- spectral_imag: bfloat16 [256, 96, 1024], P(None, 'ch', 'rows'), may hold values from -4 to 4
- query_weight: bfloat16 [96, 128], P('ch'), may hold values from -0.625 to 0.625
- key_weight: bfloat16 [96, 128], P('ch'), may hold values from -0.625 to 0.625
- query_pixels: int32 [4096], P('rows'), may hold values from 0 to 8191
- key_pixels: int32 [16384], P('rows'), may hold values from 0 to 8191
- positives: int32 [4096], P('rows'), may hold values from 0 to 16383
Outputs:
- encoded: bfloat16 [256, 96, 2048], P('rows', 'ch')
- losses: float32 [4096], P(('rows', 'ch'))
The draws below stay inside these ranges and needn't reach their ends.
Inputs may be any that keep to these rules, and one draw needn't show every extreme that they name: `query_pixels`: each entry is r * 2048 + x for a pixel at row r and column x of the query's own slab of 4 rows. `key_pixels`: each entry is r * 2048 + x for a pixel at row r and column x of the key's own slab of 4 rows. `positives`: the number of the positive key among all 16384 keys, numbered slab by slab in the order of key_pixels.
All inputs are finite; a program needn't handle non-finite values.
Results may differ from the reference program's by a relative error of at most 0.0065.
Values may be sent and summed in bfloat16 or wider, within the bound.
A program may use at most 64 MiB of HBM per device.

```python
import jax
import jax.numpy as jnp
from jax import lax

CHANNELS = 96
COLS = 2048
KEY_DIM = 128
DILATION = 2
ROWS_DEV = 4
Q_DEV = 64
K_DEV = 256
HEIGHT = 256
HALF = 1024
QUERIES = 4096
KEYS = 16384
N_ROWS = 64


def set_ends(entries, key, least, top_value):
    index_at = [jax.random.randint(jax.random.fold_in(key, axis), (), 0, length) for axis, length in enumerate(entries.shape)]
    longest = entries.shape.index(max(entries.shape))
    neighbour = index_at[:longest] + [(index_at[longest] + 1) % entries.shape[longest]] + index_at[longest + 1:]
    return entries.at[tuple(index_at)].set(least).at[tuple(neighbour)].set(top_value)


def levels(key, extent, split, low, high):
    def one(axis_at, parts):
        draws = jax.random.uniform(jax.random.fold_in(jax.random.fold_in(key, 6), axis_at), (parts,), jnp.float32, low / len(split), high / len(split))
        return jnp.repeat(jnp.exp(draws), extent[axis_at] // parts).reshape((-1,) + (1,) * (len(extent) - axis_at - 1))

    loudness = one(*split[0])
    for cut in split[1:]:
        loudness = loudness * one(*cut)
    return loudness


def scatter_about(key, shape, deviation, reach, shards=(), held_as=jnp.bfloat16):
    result = deviation * jax.random.normal(key, shape, jnp.float32)
    if shards:
        result = result * levels(key, shape, shards, -0.22, 0.18)
    return jnp.clip(result, -reach, reach).astype(held_as)


def setup_inputs(seed: int = 0) -> dict:
    key_list = jax.random.split(jax.random.key(seed), 11)
    pixels = scatter_about(key_list[0], (HEIGHT, CHANNELS, COLS), 1.0, 6.0, ((0, 64), (1, 4)))
    depth_weight = scatter_about(key_list[1], (CHANNELS, 9), 9 ** -0.5, 2.0, ((0, 4),), jnp.float32)
    mix_weight = scatter_about(key_list[2], (CHANNELS, CHANNELS), CHANNELS ** -0.5, 0.625)
    spectral_real = scatter_about(key_list[3], (HEIGHT, CHANNELS, HALF), 0.7, 4.0, ((1, 4), (2, 64)))
    spectral_imag = scatter_about(key_list[4], (HEIGHT, CHANNELS, HALF), 0.7, 4.0, ((1, 4), (2, 64)))
    query_weight = scatter_about(key_list[5], (CHANNELS, KEY_DIM), CHANNELS ** -0.5, 0.625, ((0, 4),))
    key_weight = scatter_about(key_list[6], (CHANNELS, KEY_DIM), CHANNELS ** -0.5, 0.625, ((0, 4),))
    query_pixels = set_ends(jax.random.randint(key_list[7], (QUERIES,), 0, ROWS_DEV * COLS), jax.random.fold_in(key_list[7], 1), 0, (ROWS_DEV * COLS) - 1).astype(jnp.int32)
    key_pixels = set_ends(jax.random.randint(key_list[8], (KEYS,), 0, ROWS_DEV * COLS), jax.random.fold_in(key_list[8], 1), 0, (ROWS_DEV * COLS) - 1).astype(jnp.int32)
    positives = set_ends(jax.random.randint(key_list[9], (QUERIES,), 0, KEYS), jax.random.fold_in(key_list[9], 1), 0, KEYS - 1).astype(jnp.int32)
    return {"pixels": pixels, "depth_weight": depth_weight, "mix_weight": mix_weight, "spectral_real": spectral_real, "spectral_imag": spectral_imag, "query_weight": query_weight, "key_weight": key_weight, "query_pixels": query_pixels, "key_pixels": key_pixels, "positives": positives}


score_scale = 10.0

def unit_rows(values):
    return values * lax.rsqrt(lax.optimization_barrier(jnp.sum(values * values, axis=1, keepdims=True)) + 1e-06)

def rounded(values):
    return lax.optimization_barrier(values.astype(jnp.bfloat16)).astype(jnp.float32)

def reference(pixels, depth_weight, mix_weight, spectral_real, spectral_imag, query_weight, key_weight, query_pixels, key_pixels, positives):
    padded = jnp.pad(pixels, ((DILATION, DILATION), (0, 0), (DILATION, DILATION)))

    def one_row(row_index):
        window = lax.dynamic_slice_in_dim(padded, row_index, 2 * DILATION + 1, 0)
        summed = window[DILATION, :, DILATION:DILATION + COLS].astype(jnp.float32)
        for tap_row in range(3):
            for tap_col in range(3):
                shifted = window[tap_row * DILATION, :, tap_col * DILATION:tap_col * DILATION + COLS].astype(jnp.float32)
                summed = summed + depth_weight[:, 3 * tap_row + tap_col][:, None] * shifted
        conv_out = summed.astype(jnp.bfloat16)
        mixture = jnp.dot(mix_weight.T, conv_out, preferred_element_type=jnp.float32)
        return jax.nn.gelu(mixture).astype(jnp.bfloat16)
    hidden = lax.map(one_row, jnp.arange(HEIGHT, dtype=jnp.int32))
    weights = jnp.where(jnp.arange(HALF) == 0, 1.0, 2.0)

    def one_channel(channel):
        channel_plane = lax.dynamic_index_in_dim(hidden, channel, 1, keepdims=False)
        kernel_real = lax.dynamic_index_in_dim(spectral_real, channel, 1, keepdims=False).astype(jnp.float32)
        kernel_imag = lax.dynamic_index_in_dim(spectral_imag, channel, 1, keepdims=False).astype(jnp.float32)
        along_cols = jnp.fft.fft(channel_plane.astype(jnp.float32), axis=1)[:, :HALF]
        wire_real = rounded(jnp.real(along_cols))
        wire_imag = rounded(jnp.imag(along_cols))
        spectrum = jnp.fft.fft(wire_real + 1j * wire_imag, axis=0)
        product = spectrum * (kernel_real + 1j * kernel_imag)
        back_rows = jnp.fft.ifft(product, axis=0)
        back_real = rounded(jnp.real(back_rows)) * weights[None, :]
        back_imag = rounded(jnp.imag(back_rows)) * weights[None, :]
        full_back = jnp.pad(back_real + 1j * back_imag, ((0, 0), (0, COLS - HALF)))
        spatial = jnp.real(jnp.fft.ifft(full_back, axis=1))
        return (channel_plane.astype(jnp.float32) + spatial).astype(jnp.bfloat16)
    encoded = jnp.moveaxis(lax.map(one_channel, jnp.arange(CHANNELS, dtype=jnp.int32)), 0, 1)
    key_slab = jnp.arange(KEYS, dtype=jnp.int32) // K_DEV
    key_features = encoded[key_slab * ROWS_DEV + key_pixels // COLS, :, key_pixels % COLS]
    key_unit = unit_rows(jnp.dot(key_features, key_weight, preferred_element_type=jnp.float32)).astype(jnp.bfloat16)
    query_slab = jnp.arange(QUERIES, dtype=jnp.int32) // Q_DEV
    query_features = encoded[query_slab * ROWS_DEV + query_pixels // COLS, :, query_pixels % COLS]
    query_unit = unit_rows(jnp.dot(query_features, query_weight, preferred_element_type=jnp.float32)).astype(jnp.bfloat16)

    def one_block(block_index):
        block_queries = lax.dynamic_slice_in_dim(query_unit, block_index * Q_DEV, Q_DEV, 0)
        block_targets = lax.dynamic_slice_in_dim(positives, block_index * Q_DEV, Q_DEV, 0)
        scores = jnp.dot(block_queries, key_unit.T, preferred_element_type=jnp.float32) * score_scale
        log_totals = jnp.log(lax.optimization_barrier(jnp.sum(jnp.exp(scores), axis=1)))
        picked = jnp.take_along_axis(scores, block_targets[:, None], axis=1)[:, 0]
        return log_totals - picked
    losses = lax.map(one_block, jnp.arange(N_ROWS, dtype=jnp.int32)).reshape(QUERIES)
    return (encoded, losses)
```

```python
import jax
import jax.numpy as jnp
from jax import lax
from jax.sharding import PartitionSpec as P

DILATION = 2


score_scale = 10.0
exact = lax.Precision.HIGHEST


def extended(cells, sides, width):
    for axis, dim in sides:
        count = lax.axis_size(axis)
        ends = count - 1
        head = lax.slice_in_dim(cells, 0, width, axis=dim)
        tail = lax.slice_in_dim(cells, cells.shape[dim] - width, cells.shape[dim], axis=dim)
        cells = jnp.concatenate(
            [
                lax.ppermute(tail, axis, [(i, (i + 1) % count) for i in range(ends)]),
                cells,
                lax.ppermute(head, axis, [((i + 1) % count, i) for i in range(ends)]),
            ],
            axis=dim,
        )
    return cells


def unit_rows(values):
    return values * lax.rsqrt(jnp.sum(values * values, axis=1, keepdims=True) + 1e-06)


def angle_table(left_len, right_len, length, direction):
    left_index = lax.broadcasted_iota(jnp.int32, (left_len, right_len), 0)
    right_index = lax.broadcasted_iota(jnp.int32, (left_len, right_len), 1)
    phase_turns = left_index * right_index % length
    angles = phase_turns.astype(jnp.float32) * (direction * 2.0 * jnp.pi / length)
    return (jnp.cos(angles), jnp.sin(angles))


def transform_last(real_part, imag_part, direction, real_only, lower_half):
    length = real_part.shape[-1]
    first_len = 1 << (length.bit_length() - 1) // 2
    second = length // first_len
    kept = second // 2 if lower_half else second
    leading = real_part.shape[:-1]
    cos_first, sin_first = angle_table(first_len, first_len, first_len, direction)
    cos_twist, sin_twist = angle_table(first_len, second, length, direction)
    cos_second, sin_second = angle_table(second, second, second, direction)
    cos_second = cos_second[:, :kept]
    sin_second = sin_second[:, :kept]

    def over_first(matrix, values):
        return jnp.einsum("ka,...ab->...kb", matrix, values, precision=exact)

    def over_second(values, matrix):
        return jnp.einsum("...kb,bm->...km", values, matrix, precision=exact)

    real_grid = real_part.reshape(leading + (first_len, second))
    if imag_part is None:
        segment_real = over_first(cos_first, real_grid)
        segment_imag = over_first(sin_first, real_grid)
    else:
        imag_grid = imag_part.reshape(leading + (first_len, second))
        segment_real = over_first(cos_first, real_grid) - over_first(sin_first, imag_grid)
        segment_imag = over_first(sin_first, real_grid) + over_first(cos_first, imag_grid)
    twisted_real = segment_real * cos_twist - segment_imag * sin_twist
    twisted_imag = segment_real * sin_twist + segment_imag * cos_twist
    result_real = over_second(twisted_real, cos_second) - over_second(twisted_imag, sin_second)
    result_real = jnp.swapaxes(result_real, -1, -2).reshape(leading + (kept * first_len,))
    if real_only:
        return result_real
    result_imag = over_second(twisted_real, sin_second) + over_second(twisted_imag, cos_second)
    result_imag = jnp.swapaxes(result_imag, -1, -2).reshape(leading + (kept * first_len,))
    return (result_real, result_imag)


def transform_first(real_part, imag_part, direction):
    moved_real = jnp.moveaxis(real_part, 0, -1)
    moved_imag = jnp.moveaxis(imag_part, 0, -1)
    result_real, result_imag = transform_last(moved_real, moved_imag, direction, False, False)
    return (jnp.moveaxis(result_real, -1, 0), jnp.moveaxis(result_imag, -1, 0))


def score_fold(query_unit, targets, key_number):

    def add_block(carried, shard_piece, offset):
        scores = (
            jnp.einsum("qd,kd->qk", query_unit, shard_piece, preferred_element_type=jnp.float32)
            * score_scale
        )
        numbers = key_number(lax.broadcasted_iota(jnp.int32, (1, shard_piece.shape[0]), 1))
        exp_sums = jnp.sum(jnp.exp(scores), axis=1)
        picked = jnp.sum(jnp.where(targets[:, None] == numbers, scores, 0.0), axis=1)
        return (exp_sums, picked)

    return add_block


def same_number(gathered):
    return gathered


def body(
    pixels,
    depth_weight,
    mix_weight,
    spectral_real,
    spectral_imag,
    query_weight,
    key_weight,
    query_pixels,
    key_pixels,
    positives,
):
    slab_rows, groups, columns = pixels.shape
    half_cols = columns // 2
    channel = lax.axis_index("ch")
    group_count = lax.axis_size("ch")
    padded = extended(pixels, (("rows", 0),), DILATION)
    padded = jnp.pad(padded, ((0, 0), (0, 0), (DILATION, DILATION)))
    summed = pixels.astype(jnp.float32)
    for tap_row in range(3):
        for tap_col in range(3):
            shifted = padded[
                tap_row * DILATION : tap_row * DILATION + slab_rows,
                :,
                tap_col * DILATION : tap_col * DILATION + columns,
            ]
            summed = summed + depth_weight[:, 3 * tap_row + tap_col][
                None, :, None
            ] * shifted.astype(jnp.float32)
    conv_out = summed.astype(jnp.bfloat16)
    local_columns = lax.dynamic_slice_in_dim(mix_weight, channel * groups, groups, 1)
    mixture = jnp.einsum(
        "rcw,cd->rdw",
        lax.all_gather(conv_out, "ch", axis=1, tiled=True),
        local_columns,
        preferred_element_type=jnp.float32,
    )
    hidden = jax.nn.gelu(mixture).astype(jnp.bfloat16)
    spectrum_real, spectrum_imag = transform_last(
        hidden.astype(jnp.float32), None, -1.0, False, True
    )
    wire = jnp.stack([spectrum_real, spectrum_imag]).astype(jnp.bfloat16)
    columns_both = lax.all_to_all(wire, "rows", split_axis=3, concat_axis=1, tiled=True)
    column_real, column_imag = columns_both[0], columns_both[1]
    full_real, full_imag = transform_first(
        column_real.astype(jnp.float32), column_imag.astype(jnp.float32), -1.0
    )
    kernel_real = spectral_real.astype(jnp.float32)
    kernel_imag = spectral_imag.astype(jnp.float32)
    product_real = full_real * kernel_real - full_imag * kernel_imag
    product_imag = full_real * kernel_imag + full_imag * kernel_real
    back_real, back_imag = transform_first(product_real, product_imag, 1.0)
    height = column_real.shape[0]
    back_real = (back_real * (1.0 / height)).astype(jnp.bfloat16)
    back_imag = (back_imag * (1.0 / height)).astype(jnp.bfloat16)
    rows_both = lax.all_to_all(
        jnp.stack([back_real, back_imag]), "rows", split_axis=1, concat_axis=3, tiled=True
    )
    row_real, row_imag = rows_both[0], rows_both[1]
    doubling = jnp.where(lax.broadcasted_iota(jnp.int32, (1, 1, half_cols), 2) == 0, 1.0, 2.0)
    wide_real = jnp.pad(
        row_real.astype(jnp.float32) * doubling, ((0, 0), (0, 0), (0, columns - half_cols))
    )
    wide_imag = jnp.pad(
        row_imag.astype(jnp.float32) * doubling, ((0, 0), (0, 0), (0, columns - half_cols))
    )
    spatial = transform_last(wide_real, wide_imag, 1.0, True, False) * (1.0 / columns)
    encoded = (hidden.astype(jnp.float32) + spatial).astype(jnp.bfloat16)
    key_count = key_pixels.shape[0]
    query_count = query_pixels.shape[0]
    quarter = query_count // group_count
    slab = lax.axis_index("rows")
    weights_all = lax.all_gather(
        jnp.concatenate([key_weight, query_weight], axis=1), "ch", axis=0, tiled=True
    )
    sampled = jnp.concatenate([key_pixels, query_pixels])
    features = encoded[sampled // columns, :, sampled % columns]
    features = lax.all_gather(features, "ch", axis=1, tiled=True)
    key_dim = key_weight.shape[1]
    key_unit = unit_rows(
        jnp.dot(features[:key_count], weights_all[:, :key_dim], preferred_element_type=jnp.float32)
    ).astype(jnp.bfloat16)
    own_queries = lax.dynamic_slice_in_dim(features, key_count + channel * quarter, quarter, 0)
    query_unit = unit_rows(
        jnp.dot(own_queries, weights_all[:, key_dim:], preferred_element_type=jnp.float32)
    ).astype(jnp.bfloat16)
    targets = lax.dynamic_slice_in_dim(positives, channel * quarter, quarter, 0)
    coded = jnp.concatenate([targets // 128, targets % 128]).astype(jnp.bfloat16)
    coded = jnp.pad(coded, (0, key_dim - 2 * quarter))[None, :]
    packet = jnp.concatenate([query_unit, coded], axis=0)
    gathered = lax.all_gather(packet[None], "rows", axis=0, tiled=True)
    all_queries = gathered[:, :quarter, :].reshape(-1, key_dim)
    coded_all = gathered[:, quarter, :].astype(jnp.int32)
    all_targets = (coded_all[:, :quarter] * 128 + coded_all[:, quarter : 2 * quarter]).reshape(-1)
    scores = (
        jnp.einsum("qd,kd->qk", all_queries, key_unit, preferred_element_type=jnp.float32)
        * score_scale
    )
    numbers = slab * key_count + lax.broadcasted_iota(jnp.int32, (1, key_count), 1)
    exp_sums = jnp.sum(jnp.exp(scores), axis=1)
    picked = jnp.sum(jnp.where(all_targets[:, None] == numbers, scores, 0.0), axis=1)
    reduced = lax.psum_scatter(
        jnp.stack([exp_sums, picked], axis=1), "rows", scatter_dimension=0, tiled=True
    )
    losses = jnp.log(reduced[:, 0]) - reduced[:, 1]
    return (encoded, losses)


def solution(mesh):
    placed = (
        P("rows", "ch", None),
        P("ch", None),
        P(),
        P(None, "ch", "rows"),
        P(None, "ch", "rows"),
        P("ch", None),
        P("ch", None),
        P("rows"),
        P("rows"),
        P("rows"),
    )
    return jax.shard_map(
        body,
        mesh=mesh,
        in_specs=placed,
        out_specs=(P("rows", "ch", None), P(("rows", "ch"))),
        check_vma=False,
    )
```

```python
import jax
import jax.numpy as jnp
from jax import lax
from jax.sharding import PartitionSpec as P

DILATION = 2


score_scale = 10.0
exact = lax.Precision.HIGHEST


def extended(cells, sides, width):
    for axis, dim in sides:
        count = lax.axis_size(axis)
        ends = count - 1
        head = lax.slice_in_dim(cells, 0, width, axis=dim)
        tail = lax.slice_in_dim(cells, cells.shape[dim] - width, cells.shape[dim], axis=dim)
        cells = jnp.concatenate(
            [
                lax.ppermute(tail, axis, [(i, (i + 1) % count) for i in range(ends)]),
                cells,
                lax.ppermute(head, axis, [((i + 1) % count, i) for i in range(ends)]),
            ],
            axis=dim,
        )
    return cells


def ring_pieces(values, axis):
    count = lax.axis_size(axis)
    pieces = [values]
    for shift in range(1, count):
        pieces.append(
            lax.ppermute(values, axis, [(i, (i + shift) % count) for i in range(count)])
        )
    return pieces


def unit_rows(values):
    return values * lax.rsqrt(jnp.sum(values * values, axis=1, keepdims=True) + 1e-06)


def angle_table(left_len, right_len, length, direction):
    left_index = lax.broadcasted_iota(jnp.int32, (left_len, right_len), 0)
    right_index = lax.broadcasted_iota(jnp.int32, (left_len, right_len), 1)
    phase_turns = left_index * right_index % length
    angles = phase_turns.astype(jnp.float32) * (direction * 2.0 * jnp.pi / length)
    return (jnp.cos(angles), jnp.sin(angles))


def transform_last(real_part, imag_part, direction, real_only, lower_half):
    length = real_part.shape[-1]
    first_len = 1 << (length.bit_length() - 1) // 2
    second = length // first_len
    kept = second // 2 if lower_half else second
    leading = real_part.shape[:-1]
    cos_first, sin_first = angle_table(first_len, first_len, first_len, direction)
    cos_twist, sin_twist = angle_table(first_len, second, length, direction)
    cos_second, sin_second = angle_table(second, second, second, direction)
    cos_second = cos_second[:, :kept]
    sin_second = sin_second[:, :kept]

    def over_first(matrix, values):
        return jnp.einsum("ka,...ab->...kb", matrix, values, precision=exact)

    def over_second(values, matrix):
        return jnp.einsum("...kb,bm->...km", values, matrix, precision=exact)

    real_grid = real_part.reshape(leading + (first_len, second))
    if imag_part is None:
        segment_real = over_first(cos_first, real_grid)
        segment_imag = over_first(sin_first, real_grid)
    else:
        imag_grid = imag_part.reshape(leading + (first_len, second))
        segment_real = over_first(cos_first, real_grid) - over_first(sin_first, imag_grid)
        segment_imag = over_first(sin_first, real_grid) + over_first(cos_first, imag_grid)
    twisted_real = segment_real * cos_twist - segment_imag * sin_twist
    twisted_imag = segment_real * sin_twist + segment_imag * cos_twist
    result_real = over_second(twisted_real, cos_second) - over_second(twisted_imag, sin_second)
    result_real = jnp.swapaxes(result_real, -1, -2).reshape(leading + (kept * first_len,))
    if real_only:
        return result_real
    result_imag = over_second(twisted_real, sin_second) + over_second(twisted_imag, cos_second)
    result_imag = jnp.swapaxes(result_imag, -1, -2).reshape(leading + (kept * first_len,))
    return (result_real, result_imag)


def transform_first(real_part, imag_part, direction):
    moved_real = jnp.moveaxis(real_part, 0, -1)
    moved_imag = jnp.moveaxis(imag_part, 0, -1)
    result_real, result_imag = transform_last(moved_real, moved_imag, direction, False, False)
    return (jnp.moveaxis(result_real, -1, 0), jnp.moveaxis(result_imag, -1, 0))


def score_fold(query_unit, targets, key_number):

    def add_block(carried, shard_piece, offset):
        scores = (
            jnp.einsum("qd,kd->qk", query_unit, shard_piece, preferred_element_type=jnp.float32)
            * score_scale
        )
        numbers = key_number(lax.broadcasted_iota(jnp.int32, (1, shard_piece.shape[0]), 1))
        exp_sums = jnp.sum(jnp.exp(scores), axis=1)
        picked = jnp.sum(jnp.where(targets[:, None] == numbers, scores, 0.0), axis=1)
        return (exp_sums, picked)

    return add_block


def same_number(gathered):
    return gathered


def body(
    pixels,
    depth_weight,
    mix_weight,
    spectral_real,
    spectral_imag,
    query_weight,
    key_weight,
    query_pixels,
    key_pixels,
    positives,
):
    slab_rows, groups, columns = pixels.shape
    half_cols = columns // 2
    channel = lax.axis_index("ch")
    group_count = lax.axis_size("ch")
    padded = extended(pixels, (("rows", 0),), DILATION)
    padded = jnp.pad(padded, ((0, 0), (0, 0), (DILATION, DILATION)))
    summed = pixels.astype(jnp.float32)
    for tap_row in range(3):
        for tap_col in range(3):
            shifted = padded[
                tap_row * DILATION : tap_row * DILATION + slab_rows,
                :,
                tap_col * DILATION : tap_col * DILATION + columns,
            ]
            summed = summed + depth_weight[:, 3 * tap_row + tap_col][
                None, :, None
            ] * shifted.astype(jnp.float32)
    conv_out = summed.astype(jnp.bfloat16)
    local_columns = lax.dynamic_slice_in_dim(mix_weight, channel * groups, groups, 1)
    ordered_rows = jnp.concatenate(
        [
            lax.dynamic_slice_in_dim(
                local_columns, (channel - shift) % group_count * groups, groups, 0
            )
            for shift in range(group_count)
        ],
        axis=0,
    )
    mixture = jnp.einsum(
        "rcw,cd->rdw",
        jnp.concatenate(ring_pieces(conv_out, "ch"), axis=1),
        ordered_rows,
        preferred_element_type=jnp.float32,
    )
    hidden = jax.nn.gelu(mixture).astype(jnp.bfloat16)
    spectrum_real, spectrum_imag = transform_last(
        hidden.astype(jnp.float32), None, -1.0, False, True
    )
    wire = jnp.stack([spectrum_real, spectrum_imag]).astype(jnp.bfloat16)
    columns_both = lax.all_to_all(wire, "rows", split_axis=3, concat_axis=1, tiled=True)
    column_real, column_imag = columns_both[0], columns_both[1]
    full_real, full_imag = transform_first(
        column_real.astype(jnp.float32), column_imag.astype(jnp.float32), -1.0
    )
    kernel_real = spectral_real.astype(jnp.float32)
    kernel_imag = spectral_imag.astype(jnp.float32)
    product_real = full_real * kernel_real - full_imag * kernel_imag
    product_imag = full_real * kernel_imag + full_imag * kernel_real
    back_real, back_imag = transform_first(product_real, product_imag, 1.0)
    height = column_real.shape[0]
    back_real = (back_real * (1.0 / height)).astype(jnp.bfloat16)
    back_imag = (back_imag * (1.0 / height)).astype(jnp.bfloat16)
    rows_both = lax.all_to_all(
        jnp.stack([back_real, back_imag]), "rows", split_axis=1, concat_axis=3, tiled=True
    )
    row_real, row_imag = rows_both[0], rows_both[1]
    doubling = jnp.where(lax.broadcasted_iota(jnp.int32, (1, 1, half_cols), 2) == 0, 1.0, 2.0)
    wide_real = jnp.pad(
        row_real.astype(jnp.float32) * doubling, ((0, 0), (0, 0), (0, columns - half_cols))
    )
    wide_imag = jnp.pad(
        row_imag.astype(jnp.float32) * doubling, ((0, 0), (0, 0), (0, columns - half_cols))
    )
    spatial = transform_last(wide_real, wide_imag, 1.0, True, False) * (1.0 / columns)
    encoded = (hidden.astype(jnp.float32) + spatial).astype(jnp.bfloat16)
    key_count = key_pixels.shape[0]
    query_count = query_pixels.shape[0]
    quarter = query_count // group_count
    slab = lax.axis_index("rows")
    weights_all = jnp.concatenate(
        ring_pieces(jnp.concatenate([key_weight, query_weight], axis=1), "ch"), axis=0
    )
    sampled = jnp.concatenate([key_pixels, query_pixels])
    features = encoded[sampled // columns, :, sampled % columns]
    features = jnp.concatenate(ring_pieces(features, "ch"), axis=1)
    key_dim = key_weight.shape[1]
    key_unit = unit_rows(
        jnp.dot(features[:key_count], weights_all[:, :key_dim], preferred_element_type=jnp.float32)
    ).astype(jnp.bfloat16)
    own_queries = lax.dynamic_slice_in_dim(features, key_count + channel * quarter, quarter, 0)
    query_unit = unit_rows(
        jnp.dot(own_queries, weights_all[:, key_dim:], preferred_element_type=jnp.float32)
    ).astype(jnp.bfloat16)
    targets = lax.dynamic_slice_in_dim(positives, channel * quarter, quarter, 0)
    coded = jnp.concatenate([targets // 128, targets % 128]).astype(jnp.bfloat16)
    coded = jnp.pad(coded, (0, key_dim - 2 * quarter))[None, :]
    packet = jnp.concatenate([query_unit, coded], axis=0)
    slabs = lax.axis_size("rows")
    gathered = lax.all_to_all(
        jnp.broadcast_to(packet[None], (slabs,) + packet.shape),
        "rows",
        split_axis=0,
        concat_axis=0,
        tiled=True,
    )
    all_queries = gathered[:, :quarter, :].reshape(-1, key_dim)
    coded_all = gathered[:, quarter, :].astype(jnp.int32)
    all_targets = (coded_all[:, :quarter] * 128 + coded_all[:, quarter : 2 * quarter]).reshape(-1)
    scores = (
        jnp.einsum("qd,kd->qk", all_queries, key_unit, preferred_element_type=jnp.float32)
        * score_scale
    )
    numbers = slab * key_count + lax.broadcasted_iota(jnp.int32, (1, key_count), 1)
    exp_sums = jnp.sum(jnp.exp(scores), axis=1)
    picked = jnp.sum(jnp.where(all_targets[:, None] == numbers, scores, 0.0), axis=1)
    reduced = lax.all_to_all(
        jnp.stack([exp_sums, picked], axis=1).reshape(slabs, quarter, 2),
        "rows",
        split_axis=0,
        concat_axis=0,
        tiled=True,
    ).sum(axis=0)
    losses = jnp.log(reduced[:, 0]) - reduced[:, 1]
    return (encoded, losses)


def solution(mesh):
    placed = (
        P("rows", "ch", None),
        P("ch", None),
        P(),
        P(None, "ch", "rows"),
        P(None, "ch", "rows"),
        P("ch", None),
        P("ch", None),
        P("rows"),
        P("rows"),
        P("rows"),
    )
    return jax.shard_map(
        body,
        mesh=mesh,
        in_specs=placed,
        out_specs=(P("rows", "ch", None), P(("rows", "ch"))),
        check_vma=False,
    )
```

```python
import jax
import jax.numpy as jnp
from jax import lax
from jax.sharding import PartitionSpec as P

DILATION = 2


score_scale = 10.0
exact = lax.Precision.HIGHEST


def extended(cells, sides, width):
    for axis, dim in sides:
        count = lax.axis_size(axis)
        ends = count - 1
        head = lax.slice_in_dim(cells, 0, width, axis=dim)
        tail = lax.slice_in_dim(cells, cells.shape[dim] - width, cells.shape[dim], axis=dim)
        cells = jnp.concatenate(
            [
                lax.ppermute(tail, axis, [(i, (i + 1) % count) for i in range(ends)]),
                cells,
                lax.ppermute(head, axis, [((i + 1) % count, i) for i in range(ends)]),
            ],
            axis=dim,
        )
    return cells


def ring_pieces(values, axis):
    count = lax.axis_size(axis)
    pieces = [values]
    for shift in range(1, count):
        pieces.append(
            lax.ppermute(values, axis, [(i, (i + shift) % count) for i in range(count)])
        )
    return pieces


def unit_rows(values):
    return values * lax.rsqrt(jnp.sum(values * values, axis=1, keepdims=True) + 1e-06)


def cos_sin(turns, length):
    angles = turns.astype(jnp.float32) * (2.0 * jnp.pi / length)
    return (jnp.cos(angles), jnp.sin(angles))


def split_bf16(table):
    high = table.astype(jnp.bfloat16)
    low = (table - high.astype(jnp.float32)).astype(jnp.bfloat16)
    return (high, low)


def row_tables(columns, kept):
    outer = 32
    inner = columns // outer
    a = lax.broadcasted_iota(jnp.int32, (outer, kept), 0)
    k = lax.broadcasted_iota(jnp.int32, (outer, kept), 1)
    cos_a, sin_a = cos_sin(a * k % outer, outer)
    b = lax.broadcasted_iota(jnp.int32, (inner, kept), 0)
    kb = lax.broadcasted_iota(jnp.int32, (inner, kept), 1)
    cos_b, sin_b = cos_sin(b * kb % columns, columns)
    cos_a, sin_a, cos_b, sin_b = lax.optimization_barrier((cos_a, sin_a, cos_b, sin_b))
    cos_t = cos_a[:, None, :] * cos_b[None, :, :] - sin_a[:, None, :] * sin_b[None, :, :]
    sin_t = sin_a[:, None, :] * cos_b[None, :, :] + cos_a[:, None, :] * sin_b[None, :, :]
    return (split_bf16(cos_t.reshape(columns, kept)), split_bf16(sin_t.reshape(columns, kept)))


def two_pass(eq, left, right_pair):
    return sum(
        jnp.einsum(eq, left, part, preferred_element_type=jnp.float32) for part in right_pair
    )


def column_tables(height):
    m = lax.broadcasted_iota(jnp.int32, (height, height), 0)
    y = lax.broadcasted_iota(jnp.int32, (height, height), 1)
    return cos_sin(m * y % height, height)


def column_forward(real, imag, cos_t, sin_t):
    cos_pair, sin_pair = split_bf16(cos_t), split_bf16(sin_t)

    def over(pair, values):
        return sum(
            jnp.einsum("my,ycf->mcf", part, values, preferred_element_type=jnp.float32)
            for part in pair
        )

    return (over(cos_pair, real) + over(sin_pair, imag), over(cos_pair, imag) - over(sin_pair, real))


def column_inverse(real, imag, cos_t, sin_t):
    def over(table, values):
        return jnp.einsum(
            "ym,mcf->ycf", table, values, precision=exact, preferred_element_type=jnp.float32
        )

    return (over(cos_t, real) - over(sin_t, imag), over(cos_t, imag) + over(sin_t, real))


def score_fold(query_unit, targets, key_number):

    def add_block(carried, shard_piece, offset):
        scores = (
            jnp.einsum("qd,kd->qk", query_unit, shard_piece, preferred_element_type=jnp.float32)
            * score_scale
        )
        numbers = key_number(lax.broadcasted_iota(jnp.int32, (1, shard_piece.shape[0]), 1))
        exp_sums = jnp.sum(jnp.exp(scores), axis=1)
        picked = jnp.sum(jnp.where(targets[:, None] == numbers, scores, 0.0), axis=1)
        return (exp_sums, picked)

    return add_block


def same_number(gathered):
    return gathered


def body(
    pixels,
    depth_weight,
    mix_weight,
    spectral_real,
    spectral_imag,
    query_weight,
    key_weight,
    query_pixels,
    key_pixels,
    positives,
):
    slab_rows, groups, columns = pixels.shape
    half_cols = columns // 2
    channel = lax.axis_index("ch")
    group_count = lax.axis_size("ch")
    padded = extended(pixels, (("rows", 0),), DILATION)
    padded = jnp.pad(padded, ((0, 0), (0, 0), (DILATION, DILATION)))
    summed = pixels.astype(jnp.float32)
    for tap_row in range(3):
        for tap_col in range(3):
            shifted = padded[
                tap_row * DILATION : tap_row * DILATION + slab_rows,
                :,
                tap_col * DILATION : tap_col * DILATION + columns,
            ]
            summed = summed + depth_weight[:, 3 * tap_row + tap_col][
                None, :, None
            ] * shifted.astype(jnp.float32)
    conv_out = summed.astype(jnp.bfloat16)
    local_columns = lax.dynamic_slice_in_dim(mix_weight, channel * groups, groups, 1)
    ordered_rows = jnp.concatenate(
        [
            lax.dynamic_slice_in_dim(
                local_columns, (channel - shift) % group_count * groups, groups, 0
            )
            for shift in range(group_count)
        ],
        axis=0,
    )
    mixture = jnp.einsum(
        "rcw,cd->rdw",
        jnp.concatenate(ring_pieces(conv_out, "ch"), axis=1),
        ordered_rows,
        preferred_element_type=jnp.float32,
    )
    hidden = jax.nn.gelu(mixture).astype(jnp.bfloat16)
    cos_pair, sin_pair = row_tables(columns, half_cols)
    spectrum_real = two_pass("rcx,xk->rck", hidden, cos_pair)
    spectrum_imag = -two_pass("rcx,xk->rck", hidden, sin_pair)
    wire = jnp.stack([spectrum_real, spectrum_imag]).astype(jnp.bfloat16)
    columns_both = lax.all_to_all(wire, "rows", split_axis=3, concat_axis=1, tiled=True)
    height = columns_both.shape[1]
    column_cos, column_sin = column_tables(height)
    full_real, full_imag = column_forward(columns_both[0], columns_both[1], column_cos, column_sin)
    kernel_real = spectral_real.astype(jnp.float32)
    kernel_imag = spectral_imag.astype(jnp.float32)
    product_real = full_real * kernel_real - full_imag * kernel_imag
    product_imag = full_real * kernel_imag + full_imag * kernel_real
    back_real, back_imag = column_inverse(product_real, product_imag, column_cos, column_sin)
    back_real = (back_real * (1.0 / height)).astype(jnp.bfloat16)
    back_imag = (back_imag * (1.0 / height)).astype(jnp.bfloat16)
    rows_both = lax.all_to_all(
        jnp.stack([back_real, back_imag]), "rows", split_axis=1, concat_axis=3, tiled=True
    )
    doubling = jnp.where(lax.broadcasted_iota(jnp.int32, (1, 1, half_cols), 2) == 0, 1.0, 2.0)
    weighting = doubling * (1.0 / columns)
    row_real = (rows_both[0].astype(jnp.float32) * weighting).astype(jnp.bfloat16)
    row_imag = (rows_both[1].astype(jnp.float32) * weighting).astype(jnp.bfloat16)
    spatial = two_pass("rck,xk->rcx", row_real, cos_pair) - two_pass(
        "rck,xk->rcx", row_imag, sin_pair
    )
    encoded = (hidden.astype(jnp.float32) + spatial).astype(jnp.bfloat16)
    key_count = key_pixels.shape[0]
    query_count = query_pixels.shape[0]
    quarter = query_count // group_count
    slab = lax.axis_index("rows")
    weights_all = jnp.concatenate(
        ring_pieces(jnp.concatenate([key_weight, query_weight], axis=1), "ch"), axis=0
    )
    sampled = jnp.concatenate([key_pixels, query_pixels])
    features = encoded[sampled // columns, :, sampled % columns]
    features = jnp.concatenate(ring_pieces(features, "ch"), axis=1)
    key_dim = key_weight.shape[1]
    key_unit = unit_rows(
        jnp.dot(features[:key_count], weights_all[:, :key_dim], preferred_element_type=jnp.float32)
    ).astype(jnp.bfloat16)
    own_queries = lax.dynamic_slice_in_dim(features, key_count + channel * quarter, quarter, 0)
    query_unit = unit_rows(
        jnp.dot(own_queries, weights_all[:, key_dim:], preferred_element_type=jnp.float32)
    ).astype(jnp.bfloat16)
    targets = lax.dynamic_slice_in_dim(positives, channel * quarter, quarter, 0)
    coded = jnp.concatenate([targets // 128, targets % 128]).astype(jnp.bfloat16)
    coded = jnp.pad(coded, (0, key_dim - 2 * quarter))[None, :]
    packet = jnp.concatenate([query_unit, coded], axis=0)
    slabs = lax.axis_size("rows")
    gathered = lax.all_to_all(
        jnp.broadcast_to(packet[None], (slabs,) + packet.shape),
        "rows",
        split_axis=0,
        concat_axis=0,
        tiled=True,
    )
    all_queries = gathered[:, :quarter, :].reshape(-1, key_dim)
    coded_all = gathered[:, quarter, :].astype(jnp.int32)
    all_targets = (coded_all[:, :quarter] * 128 + coded_all[:, quarter : 2 * quarter]).reshape(-1)
    scores = (
        jnp.einsum("qd,kd->qk", all_queries, key_unit, preferred_element_type=jnp.float32)
        * score_scale
    )
    numbers = slab * key_count + lax.broadcasted_iota(jnp.int32, (1, key_count), 1)
    exp_sums = jnp.sum(jnp.exp(scores), axis=1)
    picked = jnp.sum(jnp.where(all_targets[:, None] == numbers, scores, 0.0), axis=1)
    reduced = lax.all_to_all(
        jnp.stack([exp_sums, picked], axis=1).reshape(slabs, quarter, 2),
        "rows",
        split_axis=0,
        concat_axis=0,
        tiled=True,
    ).sum(axis=0)
    losses = jnp.log(reduced[:, 0]) - reduced[:, 1]
    return (encoded, losses)


def solution(mesh):
    placed = (
        P("rows", "ch", None),
        P("ch", None),
        P(),
        P(None, "ch", "rows"),
        P(None, "ch", "rows"),
        P("ch", None),
        P("ch", None),
        P("rows"),
        P("rows"),
        P("rows"),
    )
    return jax.shard_map(
        body,
        mesh=mesh,
        in_specs=placed,
        out_specs=(P("rows", "ch", None), P(("rows", "ch"))),
        check_vma=False,
    )
```

```python
import jax
import jax.numpy as jnp
from jax import lax
from jax.sharding import PartitionSpec as P

DILATION = 2


score_scale = 10.0
exact = lax.Precision.HIGHEST


def extended(cells, sides, width):
    for axis, dim in sides:
        count = lax.axis_size(axis)
        ends = count - 1
        head = lax.slice_in_dim(cells, 0, width, axis=dim)
        tail = lax.slice_in_dim(cells, cells.shape[dim] - width, cells.shape[dim], axis=dim)
        cells = jnp.concatenate(
            [
                lax.ppermute(tail, axis, [(i, (i + 1) % count) for i in range(ends)]),
                cells,
                lax.ppermute(head, axis, [((i + 1) % count, i) for i in range(ends)]),
            ],
            axis=dim,
        )
    return cells


def ring_pieces(values, axis):
    count = lax.axis_size(axis)
    pieces = [values]
    for shift in range(1, count):
        pieces.append(
            lax.ppermute(values, axis, [(i, (i + shift) % count) for i in range(count)])
        )
    return pieces


def unit_rows(values):
    return values * lax.rsqrt(jnp.sum(values * values, axis=1, keepdims=True) + 1e-06)


def cos_sin(turns, length):
    angles = turns.astype(jnp.float32) * (2.0 * jnp.pi / length)
    return (jnp.cos(angles), jnp.sin(angles))


def split_bf16(table):
    high = table.astype(jnp.bfloat16)
    low = (table - high.astype(jnp.float32)).astype(jnp.bfloat16)
    return (high, low)


def row_factors(columns, kept):
    outer = 32
    inner = columns // outer
    a = lax.broadcasted_iota(jnp.int32, (outer, kept), 0)
    k = lax.broadcasted_iota(jnp.int32, (outer, kept), 1)
    cos_a, sin_a = cos_sin(a * k % outer, outer)
    b = lax.broadcasted_iota(jnp.int32, (inner, kept), 0)
    kb = lax.broadcasted_iota(jnp.int32, (inner, kept), 1)
    cos_b, sin_b = cos_sin(b * kb % columns, columns)
    return (cos_a, sin_a, cos_b, sin_b)


def row_tables(factors):
    cos_a, sin_a, cos_b, sin_b = factors
    columns = cos_a.shape[0] * cos_b.shape[0]
    kept = cos_a.shape[1]
    cos_t = cos_a[:, None, :] * cos_b[None, :, :] - sin_a[:, None, :] * sin_b[None, :, :]
    sin_t = sin_a[:, None, :] * cos_b[None, :, :] + cos_a[:, None, :] * sin_b[None, :, :]
    return (split_bf16(cos_t.reshape(columns, kept)), split_bf16(sin_t.reshape(columns, kept)))


def two_pass(eq, left, right_pair):
    return sum(
        jnp.einsum(eq, left, part, preferred_element_type=jnp.float32) for part in right_pair
    )


def column_tables(height):
    m = lax.broadcasted_iota(jnp.int32, (height, height), 0)
    y = lax.broadcasted_iota(jnp.int32, (height, height), 1)
    return cos_sin(m * y % height, height)


def column_forward(real, imag, cos_t, sin_t):
    cos_pair, sin_pair = split_bf16(cos_t), split_bf16(sin_t)

    def over(pair, values):
        return sum(
            jnp.einsum("my,yn->mn", part, values, preferred_element_type=jnp.float32)
            for part in pair
        )

    return (over(cos_pair, real) + over(sin_pair, imag), over(cos_pair, imag) - over(sin_pair, real))


def column_inverse(real, imag, cos_t, sin_t):
    def over(table, values):
        return jnp.einsum(
            "ym,mn->yn", table, values, precision=exact, preferred_element_type=jnp.float32
        )

    return (over(cos_t, real) - over(sin_t, imag), over(cos_t, imag) + over(sin_t, real))


def score_fold(query_unit, targets, key_number):

    def add_block(carried, shard_piece, offset):
        scores = (
            jnp.einsum("qd,kd->qk", query_unit, shard_piece, preferred_element_type=jnp.float32)
            * score_scale
        )
        numbers = key_number(lax.broadcasted_iota(jnp.int32, (1, shard_piece.shape[0]), 1))
        exp_sums = jnp.sum(jnp.exp(scores), axis=1)
        picked = jnp.sum(jnp.where(targets[:, None] == numbers, scores, 0.0), axis=1)
        return (exp_sums, picked)

    return add_block


def same_number(gathered):
    return gathered


def body(
    pixels,
    depth_weight,
    mix_weight,
    spectral_real,
    spectral_imag,
    query_weight,
    key_weight,
    query_pixels,
    key_pixels,
    positives,
):
    slab_rows, groups, columns = pixels.shape
    half_cols = columns // 2
    channel = lax.axis_index("ch")
    group_count = lax.axis_size("ch")
    padded = extended(pixels, (("rows", 0),), DILATION)
    padded = jnp.pad(padded, ((0, 0), (0, 0), (DILATION, DILATION)))
    summed = pixels.astype(jnp.float32)
    for tap_row in range(3):
        for tap_col in range(3):
            shifted = padded[
                tap_row * DILATION : tap_row * DILATION + slab_rows,
                :,
                tap_col * DILATION : tap_col * DILATION + columns,
            ]
            summed = summed + depth_weight[:, 3 * tap_row + tap_col][
                None, :, None
            ] * shifted.astype(jnp.float32)
    conv_out = summed.astype(jnp.bfloat16)
    conv_out, factors = lax.optimization_barrier((conv_out, row_factors(columns, half_cols)))
    local_columns = lax.dynamic_slice_in_dim(mix_weight, channel * groups, groups, 1)
    ordered_rows = jnp.concatenate(
        [
            lax.dynamic_slice_in_dim(
                local_columns, (channel - shift) % group_count * groups, groups, 0
            )
            for shift in range(group_count)
        ],
        axis=0,
    )
    mixture = jnp.einsum(
        "rcw,cd->rdw",
        jnp.concatenate(ring_pieces(conv_out, "ch"), axis=1),
        ordered_rows,
        preferred_element_type=jnp.float32,
    )
    hidden = jax.nn.gelu(mixture).astype(jnp.bfloat16)
    cos_pair, sin_pair = row_tables(factors)
    slabs = lax.axis_size("rows")
    spectrum_real = two_pass("rcx,xk->rck", hidden, cos_pair)
    spectrum_imag = -two_pass("rcx,xk->rck", hidden, sin_pair)
    width = half_cols // slabs
    wire = jnp.stack([spectrum_real, spectrum_imag]).reshape(2, slab_rows, groups, slabs, width)
    wire = jnp.transpose(wire, (0, 3, 1, 2, 4)).reshape(2, slabs, slab_rows, groups * width)
    columns_both = lax.all_to_all(
        wire.astype(jnp.bfloat16), "rows", split_axis=1, concat_axis=1, tiled=True
    ).reshape(2, slabs * slab_rows, groups * width)
    height = columns_both.shape[1]
    column_cos, column_sin = column_tables(height)
    full_real, full_imag = column_forward(columns_both[0], columns_both[1], column_cos, column_sin)
    kernel_real = spectral_real.astype(jnp.float32).reshape(height, groups * width)
    kernel_imag = spectral_imag.astype(jnp.float32).reshape(height, groups * width)
    product_real = full_real * kernel_real - full_imag * kernel_imag
    product_imag = full_real * kernel_imag + full_imag * kernel_real
    back_real, back_imag = column_inverse(product_real, product_imag, column_cos, column_sin)
    back_real = (back_real * (1.0 / height)).astype(jnp.bfloat16)
    back_imag = (back_imag * (1.0 / height)).astype(jnp.bfloat16)
    rows_both = lax.all_to_all(
        jnp.stack([back_real, back_imag]).reshape(2, slabs, slab_rows, groups * width),
        "rows",
        split_axis=1,
        concat_axis=1,
        tiled=True,
    ).reshape(2, slabs, slab_rows, groups, width)
    rows_both = jnp.transpose(rows_both, (0, 2, 3, 1, 4)).reshape(2, slab_rows, groups, half_cols)
    doubling = jnp.where(lax.broadcasted_iota(jnp.int32, (1, 1, half_cols), 2) == 0, 1.0, 2.0)
    weighting = doubling * (1.0 / columns)
    row_real = (rows_both[0].astype(jnp.float32) * weighting).astype(jnp.bfloat16)
    row_imag = (rows_both[1].astype(jnp.float32) * weighting).astype(jnp.bfloat16)
    spatial = two_pass("rck,xk->rcx", row_real, cos_pair) - two_pass(
        "rck,xk->rcx", row_imag, sin_pair
    )
    encoded = (hidden.astype(jnp.float32) + spatial).astype(jnp.bfloat16)
    key_count = key_pixels.shape[0]
    query_count = query_pixels.shape[0]
    quarter = query_count // group_count
    slab = lax.axis_index("rows")
    weights_all = jnp.concatenate(
        ring_pieces(jnp.concatenate([key_weight, query_weight], axis=1), "ch"), axis=0
    )
    sampled = jnp.concatenate([key_pixels, query_pixels])
    features = encoded[sampled // columns, :, sampled % columns]
    features = jnp.concatenate(ring_pieces(features, "ch"), axis=1)
    key_dim = key_weight.shape[1]
    key_unit = unit_rows(
        jnp.dot(features[:key_count], weights_all[:, :key_dim], preferred_element_type=jnp.float32)
    ).astype(jnp.bfloat16)
    own_queries = lax.dynamic_slice_in_dim(features, key_count + channel * quarter, quarter, 0)
    query_unit = unit_rows(
        jnp.dot(own_queries, weights_all[:, key_dim:], preferred_element_type=jnp.float32)
    ).astype(jnp.bfloat16)
    targets = lax.dynamic_slice_in_dim(positives, channel * quarter, quarter, 0)
    coded = jnp.concatenate([targets // 128, targets % 128]).astype(jnp.bfloat16)
    coded = jnp.pad(coded, (0, key_dim - 2 * quarter))[None, :]
    packet = jnp.concatenate([query_unit, coded], axis=0)
    gathered = lax.all_to_all(
        jnp.broadcast_to(packet[None], (slabs,) + packet.shape),
        "rows",
        split_axis=0,
        concat_axis=0,
        tiled=True,
    )
    all_queries = gathered[:, :quarter, :].reshape(-1, key_dim)
    coded_all = gathered[:, quarter, :].astype(jnp.int32)
    all_targets = (coded_all[:, :quarter] * 128 + coded_all[:, quarter : 2 * quarter]).reshape(-1)
    scores = (
        jnp.einsum("qd,kd->qk", all_queries, key_unit, preferred_element_type=jnp.float32)
        * score_scale
    )
    numbers = slab * key_count + lax.broadcasted_iota(jnp.int32, (1, key_count), 1)
    exp_sums = jnp.sum(jnp.exp(scores), axis=1)
    picked = jnp.sum(jnp.where(all_targets[:, None] == numbers, scores, 0.0), axis=1)
    reduced = lax.all_to_all(
        jnp.stack([exp_sums, picked], axis=1).reshape(slabs, quarter, 2),
        "rows",
        split_axis=0,
        concat_axis=0,
        tiled=True,
    ).sum(axis=0)
    losses = jnp.log(reduced[:, 0]) - reduced[:, 1]
    return (encoded, losses)


def solution(mesh):
    placed = (
        P("rows", "ch", None),
        P("ch", None),
        P(),
        P(None, "ch", "rows"),
        P(None, "ch", "rows"),
        P("ch", None),
        P("ch", None),
        P("rows"),
        P("rows"),
        P("rows"),
    )
    return jax.shard_map(
        body,
        mesh=mesh,
        in_specs=placed,
        out_specs=(P("rows", "ch", None), P(("rows", "ch"))),
        check_vma=False,
    )
```

```python
import jax
import jax.numpy as jnp
from jax import lax
from jax.sharding import PartitionSpec as P

DILATION = 2


score_scale = 10.0
exact = lax.Precision.HIGHEST


def extended(cells, sides, width):
    for axis, dim in sides:
        count = lax.axis_size(axis)
        ends = count - 1
        head = lax.slice_in_dim(cells, 0, width, axis=dim)
        tail = lax.slice_in_dim(cells, cells.shape[dim] - width, cells.shape[dim], axis=dim)
        cells = jnp.concatenate(
            [
                lax.ppermute(tail, axis, [(i, (i + 1) % count) for i in range(ends)]),
                cells,
                lax.ppermute(head, axis, [((i + 1) % count, i) for i in range(ends)]),
            ],
            axis=dim,
        )
    return cells


def ring_pieces(values, axis):
    count = lax.axis_size(axis)
    pieces = [values]
    for shift in range(1, count):
        pieces.append(
            lax.ppermute(values, axis, [(i, (i + shift) % count) for i in range(count)])
        )
    return pieces


def unit_rows(values):
    return values * lax.rsqrt(jnp.sum(values * values, axis=1, keepdims=True) + 1e-06)


def cos_sin(turns, length):
    angles = turns.astype(jnp.float32) * (2.0 * jnp.pi / length)
    return (jnp.cos(angles), jnp.sin(angles))


def split_bf16(table):
    high = table.astype(jnp.bfloat16)
    low = (table - high.astype(jnp.float32)).astype(jnp.bfloat16)
    return (high, low)


def row_factors(columns, kept):
    outer = 32
    inner = columns // outer
    a = lax.broadcasted_iota(jnp.int32, (outer, kept), 0)
    k = lax.broadcasted_iota(jnp.int32, (outer, kept), 1)
    cos_a, sin_a = cos_sin(a * k % outer, outer)
    b = lax.broadcasted_iota(jnp.int32, (inner, kept), 0)
    kb = lax.broadcasted_iota(jnp.int32, (inner, kept), 1)
    cos_b, sin_b = cos_sin(b * kb % columns, columns)
    return (cos_a, sin_a, cos_b, sin_b)


def row_tables(factors):
    cos_a, sin_a, cos_b, sin_b = factors
    columns = cos_a.shape[0] * cos_b.shape[0]
    kept = cos_a.shape[1]
    cos_t = cos_a[:, None, :] * cos_b[None, :, :] - sin_a[:, None, :] * sin_b[None, :, :]
    sin_t = sin_a[:, None, :] * cos_b[None, :, :] + cos_a[:, None, :] * sin_b[None, :, :]
    table = jnp.concatenate([cos_t, -sin_t], axis=2).reshape(columns, 2 * kept)
    return split_bf16(table)


def two_pass(eq, left, right_pair):
    return sum(
        jnp.einsum(eq, left, part, preferred_element_type=jnp.float32) for part in right_pair
    )


def column_tables(height):
    m = lax.broadcasted_iota(jnp.int32, (height, height), 0)
    y = lax.broadcasted_iota(jnp.int32, (height, height), 1)
    return cos_sin(m * y % height, height)


def block_complex(cos_t, sin_t, sign):
    return jnp.concatenate(
        [
            jnp.concatenate([cos_t, -sign * sin_t], axis=1),
            jnp.concatenate([sign * sin_t, cos_t], axis=1),
        ],
        axis=0,
    )


def score_fold(query_unit, targets, key_number):

    def add_block(carried, shard_piece, offset):
        scores = (
            jnp.einsum("qd,kd->qk", query_unit, shard_piece, preferred_element_type=jnp.float32)
            * score_scale
        )
        numbers = key_number(lax.broadcasted_iota(jnp.int32, (1, shard_piece.shape[0]), 1))
        exp_sums = jnp.sum(jnp.exp(scores), axis=1)
        picked = jnp.sum(jnp.where(targets[:, None] == numbers, scores, 0.0), axis=1)
        return (exp_sums, picked)

    return add_block


def same_number(gathered):
    return gathered


def body(
    pixels,
    depth_weight,
    mix_weight,
    spectral_real,
    spectral_imag,
    query_weight,
    key_weight,
    query_pixels,
    key_pixels,
    positives,
):
    slab_rows, groups, columns = pixels.shape
    half_cols = columns // 2
    channel = lax.axis_index("ch")
    group_count = lax.axis_size("ch")
    padded = extended(pixels, (("rows", 0),), DILATION)
    padded = jnp.pad(padded, ((0, 0), (0, 0), (DILATION, DILATION)))
    summed = pixels.astype(jnp.float32)
    for tap_row in range(3):
        for tap_col in range(3):
            shifted = padded[
                tap_row * DILATION : tap_row * DILATION + slab_rows,
                :,
                tap_col * DILATION : tap_col * DILATION + columns,
            ]
            summed = summed + depth_weight[:, 3 * tap_row + tap_col][
                None, :, None
            ] * shifted.astype(jnp.float32)
    conv_out = summed.astype(jnp.bfloat16)
    conv_out, factors = lax.optimization_barrier((conv_out, row_factors(columns, half_cols)))
    local_columns = lax.dynamic_slice_in_dim(mix_weight, channel * groups, groups, 1)
    ordered_rows = jnp.concatenate(
        [
            lax.dynamic_slice_in_dim(
                local_columns, (channel - shift) % group_count * groups, groups, 0
            )
            for shift in range(group_count)
        ],
        axis=0,
    )
    mixture = jnp.einsum(
        "rcw,cd->rdw",
        jnp.concatenate(ring_pieces(conv_out, "ch"), axis=1),
        ordered_rows,
        preferred_element_type=jnp.float32,
    )
    hidden = jax.nn.gelu(mixture).astype(jnp.bfloat16)
    table_pair = row_tables(factors)
    slabs = lax.axis_size("rows")
    spectrum = two_pass("rcx,xk->rck", hidden, table_pair)
    width = half_cols // slabs
    wire = spectrum.reshape(slab_rows, groups, 2, slabs, width)
    wire = jnp.transpose(wire, (2, 3, 0, 1, 4)).reshape(2, slabs, slab_rows, groups * width)
    columns_both = lax.all_to_all(
        wire.astype(jnp.bfloat16), "rows", split_axis=1, concat_axis=1, tiled=True
    )
    lanes = groups * width
    height = slabs * slab_rows
    column_cos, column_sin = column_tables(height)
    forward_pair = split_bf16(block_complex(column_cos, column_sin, -1.0))
    full = sum(
        jnp.einsum("my,yn->mn", part, columns_both.reshape(2 * height, lanes),
                   preferred_element_type=jnp.float32)
        for part in forward_pair
    )
    full_real, full_imag = full[:height], full[height:]
    kernel_real = spectral_real.astype(jnp.float32).reshape(height, lanes)
    kernel_imag = spectral_imag.astype(jnp.float32).reshape(height, lanes)
    product = jnp.concatenate(
        [full_real * kernel_real - full_imag * kernel_imag,
         full_real * kernel_imag + full_imag * kernel_real],
        axis=0,
    )
    back = jnp.einsum(
        "ym,mn->yn", block_complex(column_cos, column_sin, 1.0), product,
        precision=exact, preferred_element_type=jnp.float32,
    )
    back = (back * (1.0 / height)).astype(jnp.bfloat16)
    rows_both = lax.all_to_all(
        back.reshape(2, slabs, slab_rows, lanes), "rows", split_axis=1, concat_axis=1, tiled=True
    ).reshape(2, slabs, slab_rows, groups, width)
    rows_both = jnp.transpose(rows_both, (2, 3, 0, 1, 4)).reshape(slab_rows, groups, columns)
    doubling = jnp.where(lax.broadcasted_iota(jnp.int32, (1, 1, columns), 2) % half_cols == 0, 1.0, 2.0)
    weighting = doubling * (1.0 / columns)
    row_both = (rows_both.astype(jnp.float32) * weighting).astype(jnp.bfloat16)
    spatial = two_pass("rck,xk->rcx", row_both, table_pair)
    encoded = (hidden.astype(jnp.float32) + spatial).astype(jnp.bfloat16)
    key_count = key_pixels.shape[0]
    query_count = query_pixels.shape[0]
    quarter = query_count // group_count
    slab = lax.axis_index("rows")
    weights_all = jnp.concatenate([key_weight, query_weight], axis=1)
    weights_all = lax.all_to_all(
        jnp.broadcast_to(weights_all[None], (group_count,) + weights_all.shape),
        "ch", split_axis=0, concat_axis=0, tiled=True,
    ).reshape(group_count * groups, -1)
    sampled = jnp.concatenate([key_pixels, query_pixels])
    features = encoded[sampled // columns, :, sampled % columns]
    features = lax.all_to_all(
        jnp.broadcast_to(features[None], (group_count,) + features.shape),
        "ch", split_axis=0, concat_axis=0, tiled=True,
    )
    features = jnp.transpose(features, (1, 0, 2)).reshape(features.shape[1], -1)
    key_dim = key_weight.shape[1]
    key_unit = unit_rows(
        jnp.dot(features[:key_count], weights_all[:, :key_dim], preferred_element_type=jnp.float32)
    ).astype(jnp.bfloat16)
    own_queries = lax.dynamic_slice_in_dim(features, key_count + channel * quarter, quarter, 0)
    query_unit = unit_rows(
        jnp.dot(own_queries, weights_all[:, key_dim:], preferred_element_type=jnp.float32)
    ).astype(jnp.bfloat16)
    targets = lax.dynamic_slice_in_dim(positives, channel * quarter, quarter, 0)
    coded = jnp.concatenate([targets // 128, targets % 128]).astype(jnp.bfloat16)
    coded = jnp.pad(coded, (0, key_dim - 2 * quarter))[None, :]
    packet = jnp.concatenate([query_unit, coded], axis=0)
    gathered = lax.all_to_all(
        jnp.broadcast_to(packet[None], (slabs,) + packet.shape),
        "rows",
        split_axis=0,
        concat_axis=0,
        tiled=True,
    )
    all_queries = gathered[:, :quarter, :].reshape(-1, key_dim)
    coded_all = gathered[:, quarter, :].astype(jnp.int32)
    all_targets = (coded_all[:, :quarter] * 128 + coded_all[:, quarter : 2 * quarter]).reshape(-1)
    scores = (
        jnp.einsum("qd,kd->qk", all_queries, key_unit, preferred_element_type=jnp.float32)
        * score_scale
    )
    numbers = slab * key_count + lax.broadcasted_iota(jnp.int32, (1, key_count), 1)
    exp_sums = jnp.sum(jnp.exp(scores), axis=1)
    picked = jnp.sum(jnp.where(all_targets[:, None] == numbers, scores, 0.0), axis=1)
    reduced = lax.all_to_all(
        jnp.stack([exp_sums, picked], axis=1).reshape(slabs, quarter, 2),
        "rows",
        split_axis=0,
        concat_axis=0,
        tiled=True,
    ).sum(axis=0)
    losses = jnp.log(reduced[:, 0]) - reduced[:, 1]
    return (encoded, losses)


def solution(mesh):
    placed = (
        P("rows", "ch", None),
        P("ch", None),
        P(),
        P(None, "ch", "rows"),
        P(None, "ch", "rows"),
        P("ch", None),
        P("ch", None),
        P("rows"),
        P("rows"),
        P("rows"),
    )
    return jax.shard_map(
        body,
        mesh=mesh,
        in_specs=placed,
        out_specs=(P("rows", "ch", None), P(("rows", "ch"))),
        check_vma=False,
    )
```

```python
import jax
import jax.numpy as jnp
from jax import lax
from jax.sharding import PartitionSpec as P

DILATION = 2


score_scale = 10.0
exact = lax.Precision.HIGHEST


def extended(cells, sides, width):
    for axis, dim in sides:
        count = lax.axis_size(axis)
        ends = count - 1
        head = lax.slice_in_dim(cells, 0, width, axis=dim)
        tail = lax.slice_in_dim(cells, cells.shape[dim] - width, cells.shape[dim], axis=dim)
        cells = jnp.concatenate(
            [
                lax.ppermute(tail, axis, [(i, (i + 1) % count) for i in range(ends)]),
                cells,
                lax.ppermute(head, axis, [((i + 1) % count, i) for i in range(ends)]),
            ],
            axis=dim,
        )
    return cells


def ring_pieces(values, axis):
    count = lax.axis_size(axis)
    pieces = [values]
    for shift in range(1, count):
        pieces.append(
            lax.ppermute(values, axis, [(i, (i + shift) % count) for i in range(count)])
        )
    return pieces


def unit_rows(values):
    return values * lax.rsqrt(jnp.sum(values * values, axis=1, keepdims=True) + 1e-06)


def cos_sin(turns, length):
    angles = turns.astype(jnp.float32) * (2.0 * jnp.pi / length)
    return (jnp.cos(angles), jnp.sin(angles))


def split_bf16(table):
    high = table.astype(jnp.bfloat16)
    low = (table - high.astype(jnp.float32)).astype(jnp.bfloat16)
    return (high, low)


def row_factors(columns, kept):
    outer = 32
    inner = columns // outer
    a = lax.broadcasted_iota(jnp.int32, (outer, kept), 0)
    k = lax.broadcasted_iota(jnp.int32, (outer, kept), 1)
    cos_a, sin_a = cos_sin(a * k % outer, outer)
    b = lax.broadcasted_iota(jnp.int32, (inner, kept), 0)
    kb = lax.broadcasted_iota(jnp.int32, (inner, kept), 1)
    cos_b, sin_b = cos_sin(b * kb % columns, columns)
    return (cos_a, sin_a, cos_b, sin_b)


def row_tables(factors):
    cos_a, sin_a, cos_b, sin_b = factors
    columns = cos_a.shape[0] * cos_b.shape[0]
    kept = cos_a.shape[1]
    cos_t = cos_a[:, None, :] * cos_b[None, :, :] - sin_a[:, None, :] * sin_b[None, :, :]
    sin_t = sin_a[:, None, :] * cos_b[None, :, :] + cos_a[:, None, :] * sin_b[None, :, :]
    table = jnp.concatenate([cos_t, -sin_t], axis=2).reshape(columns, 2 * kept)
    return split_bf16(table)


def two_pass(eq, left, right_pair):
    return sum(
        jnp.einsum(eq, left, part, preferred_element_type=jnp.float32) for part in right_pair
    )


def column_tables(height):
    m = lax.broadcasted_iota(jnp.int32, (height, height), 0)
    y = lax.broadcasted_iota(jnp.int32, (height, height), 1)
    return cos_sin(m * y % height, height)


def block_complex(cos_t, sin_t, sign):
    return jnp.concatenate(
        [
            jnp.concatenate([cos_t, -sign * sin_t], axis=1),
            jnp.concatenate([sign * sin_t, cos_t], axis=1),
        ],
        axis=0,
    )


def score_fold(query_unit, targets, key_number):

    def add_block(carried, shard_piece, offset):
        scores = (
            jnp.einsum("qd,kd->qk", query_unit, shard_piece, preferred_element_type=jnp.float32)
            * score_scale
        )
        numbers = key_number(lax.broadcasted_iota(jnp.int32, (1, shard_piece.shape[0]), 1))
        exp_sums = jnp.sum(jnp.exp(scores), axis=1)
        picked = jnp.sum(jnp.where(targets[:, None] == numbers, scores, 0.0), axis=1)
        return (exp_sums, picked)

    return add_block


def same_number(gathered):
    return gathered


def body(
    pixels,
    depth_weight,
    mix_weight,
    spectral_real,
    spectral_imag,
    query_weight,
    key_weight,
    query_pixels,
    key_pixels,
    positives,
):
    slab_rows, groups, columns = pixels.shape
    half_cols = columns // 2
    channel = lax.axis_index("ch")
    group_count = lax.axis_size("ch")
    padded = extended(pixels, (("rows", 0),), DILATION)
    padded = jnp.pad(padded, ((0, 0), (0, 0), (DILATION, DILATION)))
    summed = pixels.astype(jnp.float32)
    for tap_row in range(3):
        for tap_col in range(3):
            shifted = padded[
                tap_row * DILATION : tap_row * DILATION + slab_rows,
                :,
                tap_col * DILATION : tap_col * DILATION + columns,
            ]
            summed = summed + depth_weight[:, 3 * tap_row + tap_col][
                None, :, None
            ] * shifted.astype(jnp.float32)
    conv_out = summed.astype(jnp.bfloat16)
    conv_out, factors = lax.optimization_barrier((conv_out, row_factors(columns, half_cols)))
    local_columns = lax.dynamic_slice_in_dim(mix_weight, channel * groups, groups, 1)
    ordered_rows = jnp.concatenate(
        [
            lax.dynamic_slice_in_dim(
                local_columns, (channel - shift) % group_count * groups, groups, 0
            )
            for shift in range(group_count)
        ],
        axis=0,
    )
    mixture = jnp.einsum(
        "rcw,cd->rdw",
        jnp.concatenate(ring_pieces(conv_out, "ch"), axis=1),
        ordered_rows,
        preferred_element_type=jnp.float32,
    )
    hidden = jax.nn.gelu(mixture).astype(jnp.bfloat16)
    table_pair = row_tables(factors)
    slabs = lax.axis_size("rows")
    spectrum = two_pass("rcx,xk->rck", hidden, table_pair)
    width = half_cols // slabs
    wire = spectrum.reshape(slab_rows, groups, 2, slabs, width)
    wire = jnp.transpose(wire, (2, 3, 0, 1, 4)).reshape(2, slabs, slab_rows, groups * width)
    columns_both = lax.all_to_all(
        wire.astype(jnp.bfloat16), "rows", split_axis=1, concat_axis=1, tiled=True
    )
    lanes = groups * width
    height = slabs * slab_rows
    column_cos, column_sin = column_tables(height)
    forward_pair = split_bf16(block_complex(column_cos, column_sin, -1.0))
    full = sum(
        jnp.einsum("my,yn->mn", part, columns_both.reshape(2 * height, lanes),
                   preferred_element_type=jnp.float32)
        for part in forward_pair
    )
    full_real, full_imag = full[:height], full[height:]
    kernel_real = spectral_real.astype(jnp.float32).reshape(height, lanes)
    kernel_imag = spectral_imag.astype(jnp.float32).reshape(height, lanes)
    product = jnp.concatenate(
        [full_real * kernel_real - full_imag * kernel_imag,
         full_real * kernel_imag + full_imag * kernel_real],
        axis=0,
    )
    back = jnp.einsum(
        "ym,mn->yn", block_complex(column_cos, column_sin, 1.0), product,
        precision=exact, preferred_element_type=jnp.float32,
    )
    back = (back * (1.0 / height)).astype(jnp.bfloat16)
    rows_both = lax.all_to_all(
        back.reshape(2, slabs, slab_rows, lanes), "rows", split_axis=1, concat_axis=1, tiled=True
    ).reshape(2, slabs, slab_rows, groups, width)
    rows_both = jnp.transpose(rows_both, (2, 3, 0, 1, 4)).reshape(slab_rows, groups, columns)
    doubling = jnp.where(lax.broadcasted_iota(jnp.int32, (1, 1, columns), 2) % half_cols == 0, 1.0, 2.0)
    weighting = doubling * (1.0 / columns)
    row_both = lax.optimization_barrier(rows_both * weighting.astype(jnp.bfloat16))
    spatial = two_pass("rck,xk->rcx", row_both, table_pair)
    encoded = (hidden.astype(jnp.float32) + spatial).astype(jnp.bfloat16)
    key_count = key_pixels.shape[0]
    query_count = query_pixels.shape[0]
    quarter = query_count // group_count
    slab = lax.axis_index("rows")
    weight_pieces = jnp.stack(ring_pieces(jnp.concatenate([key_weight, query_weight], axis=1), "ch"))
    owners = (channel - jnp.arange(group_count)) % group_count
    weights_all = jnp.take(weight_pieces, owners, axis=0).reshape(group_count * groups, -1)
    sampled = jnp.concatenate([key_pixels, query_pixels])
    features = encoded[sampled // columns, :, sampled % columns]
    features = lax.all_to_all(
        jnp.broadcast_to(features[None], (group_count,) + features.shape),
        "ch", split_axis=0, concat_axis=0, tiled=True,
    )
    features = jnp.transpose(features, (1, 0, 2)).reshape(features.shape[1], -1)
    key_dim = key_weight.shape[1]
    key_unit = unit_rows(
        jnp.dot(features[:key_count], weights_all[:, :key_dim], preferred_element_type=jnp.float32)
    ).astype(jnp.bfloat16)
    own_queries = lax.dynamic_slice_in_dim(features, key_count + channel * quarter, quarter, 0)
    query_unit = unit_rows(
        jnp.dot(own_queries, weights_all[:, key_dim:], preferred_element_type=jnp.float32)
    ).astype(jnp.bfloat16)
    targets = lax.dynamic_slice_in_dim(positives, channel * quarter, quarter, 0)
    coded = jnp.concatenate([targets // 128, targets % 128]).astype(jnp.bfloat16)
    coded = jnp.pad(coded, (0, key_dim - 2 * quarter))[None, :]
    packet = jnp.concatenate([query_unit, coded], axis=0)
    gathered = lax.all_to_all(
        jnp.broadcast_to(packet[None], (slabs,) + packet.shape),
        "rows",
        split_axis=0,
        concat_axis=0,
        tiled=True,
    )
    all_queries = gathered[:, :quarter, :].reshape(-1, key_dim)
    coded_all = gathered[:, quarter, :].astype(jnp.int32)
    all_targets = (coded_all[:, :quarter] * 128 + coded_all[:, quarter : 2 * quarter]).reshape(-1)
    scores = (
        jnp.einsum("qd,kd->qk", all_queries, key_unit, preferred_element_type=jnp.float32)
        * score_scale
    )
    numbers = slab * key_count + lax.broadcasted_iota(jnp.int32, (1, key_count), 1)
    exp_sums = jnp.sum(jnp.exp(scores), axis=1)
    picked = jnp.sum(jnp.where(all_targets[:, None] == numbers, scores, 0.0), axis=1)
    reduced = lax.all_to_all(
        jnp.stack([exp_sums, picked], axis=1).reshape(slabs, quarter, 2),
        "rows",
        split_axis=0,
        concat_axis=0,
        tiled=True,
    ).sum(axis=0)
    losses = jnp.log(reduced[:, 0]) - reduced[:, 1]
    return (encoded, losses)


def solution(mesh):
    placed = (
        P("rows", "ch", None),
        P("ch", None),
        P(),
        P(None, "ch", "rows"),
        P(None, "ch", "rows"),
        P("ch", None),
        P("ch", None),
        P("rows"),
        P("rows"),
        P("rows"),
    )
    return jax.shard_map(
        body,
        mesh=mesh,
        in_specs=placed,
        out_specs=(P("rows", "ch", None), P(("rows", "ch"))),
        check_vma=False,
    )
```

```python
import jax
import jax.numpy as jnp
from jax import lax
from jax.sharding import PartitionSpec as P

DILATION = 2


score_scale = 10.0
exact = lax.Precision.HIGHEST


def extended(cells, sides, width):
    for axis, dim in sides:
        count = lax.axis_size(axis)
        ends = count - 1
        head = lax.slice_in_dim(cells, 0, width, axis=dim)
        tail = lax.slice_in_dim(cells, cells.shape[dim] - width, cells.shape[dim], axis=dim)
        cells = jnp.concatenate(
            [
                lax.ppermute(tail, axis, [(i, (i + 1) % count) for i in range(ends)]),
                cells,
                lax.ppermute(head, axis, [((i + 1) % count, i) for i in range(ends)]),
            ],
            axis=dim,
        )
    return cells


def ring_pieces(values, axis):
    count = lax.axis_size(axis)
    pieces = [values]
    for shift in range(1, count):
        pieces.append(
            lax.ppermute(values, axis, [(i, (i + shift) % count) for i in range(count)])
        )
    return pieces


def unit_rows(values):
    return values * lax.rsqrt(jnp.sum(values * values, axis=1, keepdims=True) + 1e-06)


def cos_sin(turns, length):
    angles = turns.astype(jnp.float32) * (2.0 * jnp.pi / length)
    return (jnp.cos(angles), jnp.sin(angles))


def split_bf16(table):
    high = table.astype(jnp.bfloat16)
    low = (table - high.astype(jnp.float32)).astype(jnp.bfloat16)
    return (high, low)


def row_factors(columns, kept):
    outer = 32
    inner = columns // outer
    a = lax.broadcasted_iota(jnp.int32, (outer, kept), 0)
    k = lax.broadcasted_iota(jnp.int32, (outer, kept), 1)
    cos_a, sin_a = cos_sin(a * k % outer, outer)
    b = lax.broadcasted_iota(jnp.int32, (inner, kept), 0)
    kb = lax.broadcasted_iota(jnp.int32, (inner, kept), 1)
    cos_b, sin_b = cos_sin(b * kb % columns, columns)
    return (cos_a, sin_a, cos_b, sin_b)


def row_tables(factors):
    cos_a, sin_a, cos_b, sin_b = factors
    columns = cos_a.shape[0] * cos_b.shape[0]
    kept = cos_a.shape[1]
    cos_t = cos_a[:, None, :] * cos_b[None, :, :] - sin_a[:, None, :] * sin_b[None, :, :]
    sin_t = sin_a[:, None, :] * cos_b[None, :, :] + cos_a[:, None, :] * sin_b[None, :, :]
    table = jnp.concatenate([cos_t, -sin_t], axis=2).reshape(columns, 2 * kept)
    return split_bf16(table)


def inverse_row_tables(factors):
    cos_a, sin_a, cos_b, sin_b = (part.T for part in factors)
    columns = cos_a.shape[1] * cos_b.shape[1]
    kept = cos_a.shape[0]
    cos_t = cos_a[:, :, None] * cos_b[:, None, :] - sin_a[:, :, None] * sin_b[:, None, :]
    sin_t = sin_a[:, :, None] * cos_b[:, None, :] + cos_a[:, :, None] * sin_b[:, None, :]
    table = jnp.concatenate([cos_t, -sin_t], axis=0).reshape(2 * kept, columns)
    return split_bf16(table)


def two_pass(eq, left, right_pair):
    return sum(
        jnp.einsum(eq, left, part, preferred_element_type=jnp.float32) for part in right_pair
    )


def column_tables(height):
    m = lax.broadcasted_iota(jnp.int32, (height, height), 0)
    y = lax.broadcasted_iota(jnp.int32, (height, height), 1)
    return cos_sin(m * y % height, height)


def block_complex(cos_t, sin_t, sign):
    return jnp.concatenate(
        [
            jnp.concatenate([cos_t, -sign * sin_t], axis=1),
            jnp.concatenate([sign * sin_t, cos_t], axis=1),
        ],
        axis=0,
    )


def score_fold(query_unit, targets, key_number):

    def add_block(carried, shard_piece, offset):
        scores = (
            jnp.einsum("qd,kd->qk", query_unit, shard_piece, preferred_element_type=jnp.float32)
            * score_scale
        )
        numbers = key_number(lax.broadcasted_iota(jnp.int32, (1, shard_piece.shape[0]), 1))
        exp_sums = jnp.sum(jnp.exp(scores), axis=1)
        picked = jnp.sum(jnp.where(targets[:, None] == numbers, scores, 0.0), axis=1)
        return (exp_sums, picked)

    return add_block


def same_number(gathered):
    return gathered


def body(
    pixels,
    depth_weight,
    mix_weight,
    spectral_real,
    spectral_imag,
    query_weight,
    key_weight,
    query_pixels,
    key_pixels,
    positives,
):
    slab_rows, groups, columns = pixels.shape
    half_cols = columns // 2
    channel = lax.axis_index("ch")
    group_count = lax.axis_size("ch")
    padded = extended(pixels, (("rows", 0),), DILATION)
    padded = jnp.pad(padded, ((0, 0), (0, 0), (DILATION, DILATION)))
    summed = pixels.astype(jnp.float32)
    for tap_row in range(3):
        for tap_col in range(3):
            shifted = padded[
                tap_row * DILATION : tap_row * DILATION + slab_rows,
                :,
                tap_col * DILATION : tap_col * DILATION + columns,
            ]
            summed = summed + depth_weight[:, 3 * tap_row + tap_col][
                None, :, None
            ] * shifted.astype(jnp.float32)
    conv_out = summed.astype(jnp.bfloat16)
    conv_out, factors = lax.optimization_barrier((conv_out, row_factors(columns, half_cols)))
    local_columns = lax.dynamic_slice_in_dim(mix_weight, channel * groups, groups, 1)
    ordered_rows = jnp.concatenate(
        [
            lax.dynamic_slice_in_dim(
                local_columns, (channel - shift) % group_count * groups, groups, 0
            )
            for shift in range(group_count)
        ],
        axis=0,
    )
    mixture = jnp.einsum(
        "rcw,cd->rdw",
        jnp.concatenate(ring_pieces(conv_out, "ch"), axis=1),
        ordered_rows,
        preferred_element_type=jnp.float32,
    )
    hidden = jax.nn.gelu(mixture).astype(jnp.bfloat16)
    table_pair = row_tables(factors)
    slabs = lax.axis_size("rows")
    spectrum = two_pass("rcx,xk->rck", hidden, table_pair)
    width = half_cols // slabs
    wire = spectrum.reshape(slab_rows, groups, 2, slabs, width)
    wire = jnp.transpose(wire, (2, 3, 0, 1, 4)).reshape(2, slabs, slab_rows, groups * width)
    columns_both = lax.all_to_all(
        wire.astype(jnp.bfloat16), "rows", split_axis=1, concat_axis=1, tiled=True
    )
    lanes = groups * width
    height = slabs * slab_rows
    column_cos, column_sin = column_tables(height)
    forward_pair = split_bf16(block_complex(column_cos, column_sin, -1.0))
    full = sum(
        jnp.einsum("my,yn->mn", part, columns_both.reshape(2 * height, lanes),
                   preferred_element_type=jnp.float32)
        for part in forward_pair
    )
    full_real, full_imag = full[:height], full[height:]
    kernel_real = spectral_real.astype(jnp.float32).reshape(height, lanes)
    kernel_imag = spectral_imag.astype(jnp.float32).reshape(height, lanes)
    product = jnp.concatenate(
        [full_real * kernel_real - full_imag * kernel_imag,
         full_real * kernel_imag + full_imag * kernel_real],
        axis=0,
    )
    back = jnp.einsum(
        "ym,mn->yn", block_complex(column_cos, column_sin, 1.0), product,
        precision=exact, preferred_element_type=jnp.float32,
    )
    back = (back * (1.0 / height)).astype(jnp.bfloat16)
    rows_both = lax.all_to_all(
        back.reshape(2, slabs, slab_rows, lanes), "rows", split_axis=1, concat_axis=1, tiled=True
    ).reshape(2, slabs, slab_rows, groups, width)
    rows_both = jnp.transpose(rows_both, (2, 3, 0, 1, 4)).reshape(slab_rows, groups, columns)
    doubling = jnp.where(lax.broadcasted_iota(jnp.int32, (1, 1, columns), 2) % half_cols == 0, 1.0, 2.0)
    weighting = doubling * (1.0 / columns)
    row_both = lax.optimization_barrier(rows_both * weighting.astype(jnp.bfloat16))
    spatial = two_pass("rck,kx->rcx", row_both, inverse_row_tables(factors))
    encoded = (hidden.astype(jnp.float32) + spatial).astype(jnp.bfloat16)
    key_count = key_pixels.shape[0]
    query_count = query_pixels.shape[0]
    quarter = query_count // group_count
    slab = lax.axis_index("rows")
    weights_all = jnp.concatenate(
        ring_pieces(jnp.concatenate([key_weight, query_weight], axis=1), "ch"), axis=0
    )
    sampled = jnp.concatenate([key_pixels, query_pixels])
    features = encoded[sampled // columns, :, sampled % columns]
    features = jnp.concatenate(ring_pieces(features, "ch"), axis=1)
    key_dim = key_weight.shape[1]
    key_unit = unit_rows(
        jnp.dot(features[:key_count], weights_all[:, :key_dim], preferred_element_type=jnp.float32)
    ).astype(jnp.bfloat16)
    own_queries = lax.dynamic_slice_in_dim(features, key_count + channel * quarter, quarter, 0)
    query_unit = unit_rows(
        jnp.dot(own_queries, weights_all[:, key_dim:], preferred_element_type=jnp.float32)
    ).astype(jnp.bfloat16)
    targets = lax.dynamic_slice_in_dim(positives, channel * quarter, quarter, 0)
    coded = jnp.concatenate([targets // 128, targets % 128]).astype(jnp.bfloat16)
    coded = jnp.pad(coded, (0, key_dim - 2 * quarter))[None, :]
    packet = jnp.concatenate([query_unit, coded], axis=0)
    gathered = lax.all_to_all(
        jnp.broadcast_to(packet[None], (slabs,) + packet.shape),
        "rows",
        split_axis=0,
        concat_axis=0,
        tiled=True,
    )
    all_queries = gathered[:, :quarter, :].reshape(-1, key_dim)
    coded_all = gathered[:, quarter, :].astype(jnp.int32)
    all_targets = (coded_all[:, :quarter] * 128 + coded_all[:, quarter : 2 * quarter]).reshape(-1)
    scores = (
        jnp.einsum("qd,kd->qk", all_queries, key_unit, preferred_element_type=jnp.float32)
        * score_scale
    )
    numbers = slab * key_count + lax.broadcasted_iota(jnp.int32, (1, key_count), 1)
    exp_sums = jnp.sum(jnp.exp(scores), axis=1)
    picked = jnp.sum(jnp.where(all_targets[:, None] == numbers, scores, 0.0), axis=1)
    reduced = lax.all_to_all(
        jnp.stack([exp_sums, picked], axis=1).reshape(slabs, quarter, 2),
        "rows",
        split_axis=0,
        concat_axis=0,
        tiled=True,
    ).sum(axis=0)
    losses = jnp.log(reduced[:, 0]) - reduced[:, 1]
    return (encoded, losses)


def solution(mesh):
    placed = (
        P("rows", "ch", None),
        P("ch", None),
        P(),
        P(None, "ch", "rows"),
        P(None, "ch", "rows"),
        P("ch", None),
        P("ch", None),
        P("rows"),
        P("rows"),
        P("rows"),
    )
    return jax.shard_map(
        body,
        mesh=mesh,
        in_specs=placed,
        out_specs=(P("rows", "ch", None), P(("rows", "ch"))),
        check_vma=False,
    )
```

```python
import jax
import jax.numpy as jnp
from jax import lax
from jax.sharding import PartitionSpec as P

DILATION = 2


score_scale = 10.0
exact = lax.Precision.HIGHEST


def extended(cells, sides, width):
    for axis, dim in sides:
        count = lax.axis_size(axis)
        ends = count - 1
        head = lax.slice_in_dim(cells, 0, width, axis=dim)
        tail = lax.slice_in_dim(cells, cells.shape[dim] - width, cells.shape[dim], axis=dim)
        cells = jnp.concatenate(
            [
                lax.ppermute(tail, axis, [(i, (i + 1) % count) for i in range(ends)]),
                cells,
                lax.ppermute(head, axis, [((i + 1) % count, i) for i in range(ends)]),
            ],
            axis=dim,
        )
    return cells


def ring_pieces(values, axis):
    count = lax.axis_size(axis)
    pieces = [values]
    for shift in range(1, count):
        pieces.append(
            lax.ppermute(values, axis, [(i, (i + shift) % count) for i in range(count)])
        )
    return pieces


def unit_rows(values):
    return values * lax.rsqrt(jnp.sum(values * values, axis=1, keepdims=True) + 1e-06)


def cos_sin(turns, length):
    angles = turns.astype(jnp.float32) * (2.0 * jnp.pi / length)
    return (jnp.cos(angles), jnp.sin(angles))


def split_bf16(table):
    high = table.astype(jnp.bfloat16)
    low = (table - high.astype(jnp.float32)).astype(jnp.bfloat16)
    return (high, low)


def row_factors(columns, kept):
    outer = 32
    inner = columns // outer
    a = lax.broadcasted_iota(jnp.int32, (outer, kept), 0)
    k = lax.broadcasted_iota(jnp.int32, (outer, kept), 1)
    cos_a, sin_a = cos_sin(a * k % outer, outer)
    b = lax.broadcasted_iota(jnp.int32, (inner, kept), 0)
    kb = lax.broadcasted_iota(jnp.int32, (inner, kept), 1)
    cos_b, sin_b = cos_sin(b * kb % columns, columns)
    return (cos_a, sin_a, cos_b, sin_b)


def row_tables(factors):
    cos_a, sin_a, cos_b, sin_b = factors
    columns = cos_a.shape[0] * cos_b.shape[0]
    kept = cos_a.shape[1]
    cos_t = cos_a[:, None, :] * cos_b[None, :, :] - sin_a[:, None, :] * sin_b[None, :, :]
    sin_t = sin_a[:, None, :] * cos_b[None, :, :] + cos_a[:, None, :] * sin_b[None, :, :]
    table = jnp.concatenate([cos_t, -sin_t], axis=2).reshape(columns, 2 * kept)
    return split_bf16(table)


def two_pass(eq, left, right_pair):
    return sum(
        jnp.einsum(eq, left, part, preferred_element_type=jnp.float32) for part in right_pair
    )


def column_tables(height):
    m = lax.broadcasted_iota(jnp.int32, (height, height), 0)
    y = lax.broadcasted_iota(jnp.int32, (height, height), 1)
    return cos_sin(m * y % height, height)


def block_complex(cos_t, sin_t, sign):
    return jnp.concatenate(
        [
            jnp.concatenate([cos_t, -sign * sin_t], axis=1),
            jnp.concatenate([sign * sin_t, cos_t], axis=1),
        ],
        axis=0,
    )


def score_fold(query_unit, targets, key_number):

    def add_block(carried, shard_piece, offset):
        scores = (
            jnp.einsum("qd,kd->qk", query_unit, shard_piece, preferred_element_type=jnp.float32)
            * score_scale
        )
        numbers = key_number(lax.broadcasted_iota(jnp.int32, (1, shard_piece.shape[0]), 1))
        exp_sums = jnp.sum(jnp.exp(scores), axis=1)
        picked = jnp.sum(jnp.where(targets[:, None] == numbers, scores, 0.0), axis=1)
        return (exp_sums, picked)

    return add_block


def same_number(gathered):
    return gathered


def body(
    pixels,
    depth_weight,
    mix_weight,
    spectral_real,
    spectral_imag,
    query_weight,
    key_weight,
    query_pixels,
    key_pixels,
    positives,
):
    slab_rows, groups, columns = pixels.shape
    half_cols = columns // 2
    channel = lax.axis_index("ch")
    group_count = lax.axis_size("ch")
    padded = extended(pixels, (("rows", 0),), DILATION)
    padded = jnp.pad(padded, ((0, 0), (0, 0), (DILATION, DILATION)))
    summed = pixels.astype(jnp.float32)
    for tap_row in range(3):
        for tap_col in range(3):
            shifted = padded[
                tap_row * DILATION : tap_row * DILATION + slab_rows,
                :,
                tap_col * DILATION : tap_col * DILATION + columns,
            ]
            summed = summed + depth_weight[:, 3 * tap_row + tap_col][
                None, :, None
            ] * shifted.astype(jnp.float32)
    conv_out = summed.astype(jnp.bfloat16)
    conv_out, factors = lax.optimization_barrier((conv_out, row_factors(columns, half_cols)))
    local_columns = lax.dynamic_slice_in_dim(mix_weight, channel * groups, groups, 1)
    ordered_rows = jnp.concatenate(
        [
            lax.dynamic_slice_in_dim(
                local_columns, (channel - shift) % group_count * groups, groups, 0
            )
            for shift in range(group_count)
        ],
        axis=0,
    )
    mixture = jnp.einsum(
        "rcw,cd->rdw",
        jnp.concatenate(ring_pieces(conv_out, "ch"), axis=1),
        ordered_rows,
        preferred_element_type=jnp.float32,
    )
    hidden = jax.nn.gelu(mixture).astype(jnp.bfloat16)
    table_pair = row_tables(factors)
    slabs = lax.axis_size("rows")
    spectrum = two_pass("rcx,xk->rck", hidden, table_pair)
    width = half_cols // slabs
    wire = spectrum.reshape(slab_rows, groups, 2, slabs, width)
    wire = jnp.transpose(wire, (2, 3, 0, 1, 4)).reshape(2, slabs, slab_rows, groups * width)
    columns_both = lax.all_to_all(
        wire.astype(jnp.bfloat16), "rows", split_axis=1, concat_axis=1, tiled=True
    )
    lanes = groups * width
    height = slabs * slab_rows
    column_cos, column_sin = column_tables(height)
    forward_pair = split_bf16(block_complex(column_cos, column_sin, -1.0))
    full = sum(
        jnp.einsum("my,yn->mn", part, columns_both.reshape(2 * height, lanes),
                   preferred_element_type=jnp.float32)
        for part in forward_pair
    )
    full_real, full_imag = full[:height], full[height:]
    kernel_real = spectral_real.astype(jnp.float32).reshape(height, lanes)
    kernel_imag = spectral_imag.astype(jnp.float32).reshape(height, lanes)
    product = jnp.concatenate(
        [full_real * kernel_real - full_imag * kernel_imag,
         full_real * kernel_imag + full_imag * kernel_real],
        axis=0,
    )
    back = jnp.einsum(
        "ym,mn->yn", block_complex(column_cos, column_sin, 1.0), product,
        precision=exact, preferred_element_type=jnp.float32,
    )
    back = (back * (1.0 / height)).astype(jnp.bfloat16)
    rows_both = lax.all_to_all(
        back.reshape(2, slabs, slab_rows, lanes), "rows", split_axis=1, concat_axis=1, tiled=True
    ).reshape(2, slabs, slab_rows, groups, width)
    rows_both = jnp.transpose(rows_both, (2, 3, 0, 1, 4)).reshape(slab_rows, groups, columns)
    doubling = jnp.where(lax.broadcasted_iota(jnp.int32, (1, 1, columns), 2) % half_cols == 0, 1.0, 2.0)
    weighting = doubling * (1.0 / columns)
    row_both = lax.optimization_barrier(rows_both * weighting.astype(jnp.bfloat16))
    spatial = two_pass("rck,xk->rcx", row_both, table_pair)
    encoded = (hidden.astype(jnp.float32) + spatial).astype(jnp.bfloat16)
    key_count = key_pixels.shape[0]
    query_count = query_pixels.shape[0]
    quarter = query_count // group_count
    slab = lax.axis_index("rows")
    weights_all = jnp.concatenate(
        ring_pieces(jnp.concatenate([key_weight, query_weight], axis=1), "ch"), axis=0
    )
    sampled = jnp.concatenate([key_pixels, query_pixels])
    features = encoded[sampled // columns, :, sampled % columns]
    features = jnp.concatenate(ring_pieces(features, "ch"), axis=1)
    key_dim = key_weight.shape[1]
    key_unit = unit_rows(
        jnp.dot(features[:key_count], weights_all[:, :key_dim], preferred_element_type=jnp.float32)
    ).astype(jnp.bfloat16)
    own_queries = lax.dynamic_slice_in_dim(features, key_count + channel * quarter, quarter, 0)
    query_unit = unit_rows(
        jnp.dot(own_queries, weights_all[:, key_dim:], preferred_element_type=jnp.float32)
    ).astype(jnp.bfloat16)
    targets = lax.dynamic_slice_in_dim(positives, channel * quarter, quarter, 0)
    coded = jnp.concatenate([targets // 128, targets % 128]).astype(jnp.bfloat16)
    coded = jnp.pad(coded, (0, key_dim - 2 * quarter))[None, :]
    packet = jnp.concatenate([query_unit, coded], axis=0)
    gathered = lax.all_to_all(
        jnp.broadcast_to(packet[None], (slabs,) + packet.shape),
        "rows",
        split_axis=0,
        concat_axis=0,
        tiled=True,
    )
    all_queries = gathered[:, :quarter, :].reshape(-1, key_dim)
    coded_all = gathered[:, quarter, :].astype(jnp.int32)
    all_targets = (coded_all[:, :quarter] * 128 + coded_all[:, quarter : 2 * quarter]).reshape(-1)
    scores = (
        jnp.einsum("qd,kd->qk", all_queries, key_unit, preferred_element_type=jnp.float32)
        * score_scale
    )
    numbers = slab * key_count + lax.broadcasted_iota(jnp.int32, (1, key_count), 1)
    exp_sums = jnp.sum(jnp.exp(scores), axis=1)
    picked = jnp.sum(jnp.where(all_targets[:, None] == numbers, scores, 0.0), axis=1)
    reduced = lax.all_to_all(
        jnp.stack([exp_sums, picked], axis=1).reshape(slabs, quarter, 2),
        "rows",
        split_axis=0,
        concat_axis=0,
        tiled=True,
    ).sum(axis=0)
    losses = jnp.log(reduced[:, 0]) - reduced[:, 1]
    return (encoded, losses)


def solution(mesh):
    placed = (
        P("rows", "ch", None),
        P("ch", None),
        P(),
        P(None, "ch", "rows"),
        P(None, "ch", "rows"),
        P("ch", None),
        P("ch", None),
        P("rows"),
        P("rows"),
        P("rows"),
    )
    return jax.shard_map(
        body,
        mesh=mesh,
        in_specs=placed,
        out_specs=(P("rows", "ch", None), P(("rows", "ch"))),
        check_vma=False,
    )
```

```python
import jax
import jax.numpy as jnp
from jax import lax
from jax.sharding import PartitionSpec as P

DILATION = 2


score_scale = 10.0
exact = lax.Precision.HIGHEST


def extended(cells, sides, width):
    for axis, dim in sides:
        count = lax.axis_size(axis)
        ends = count - 1
        head = lax.slice_in_dim(cells, 0, width, axis=dim)
        tail = lax.slice_in_dim(cells, cells.shape[dim] - width, cells.shape[dim], axis=dim)
        cells = jnp.concatenate(
            [
                lax.ppermute(tail, axis, [(i, (i + 1) % count) for i in range(ends)]),
                cells,
                lax.ppermute(head, axis, [((i + 1) % count, i) for i in range(ends)]),
            ],
            axis=dim,
        )
    return cells


def ring_pieces(values, axis):
    count = lax.axis_size(axis)
    pieces = [values]
    for shift in range(1, count):
        pieces.append(
            lax.ppermute(values, axis, [(i, (i + shift) % count) for i in range(count)])
        )
    return pieces


def unit_rows(values):
    return values * lax.rsqrt(jnp.sum(values * values, axis=1, keepdims=True) + 1e-06)


def cos_sin(turns, length):
    angles = turns.astype(jnp.float32) * (2.0 * jnp.pi / length)
    return (jnp.cos(angles), jnp.sin(angles))


def split_bf16(table):
    high = table.astype(jnp.bfloat16)
    low = (table - high.astype(jnp.float32)).astype(jnp.bfloat16)
    return (high, low)


def row_factors(columns, kept):
    outer = 32
    inner = columns // outer
    a = lax.broadcasted_iota(jnp.int32, (outer, kept), 0)
    k = lax.broadcasted_iota(jnp.int32, (outer, kept), 1)
    cos_a, sin_a = cos_sin(a * k % outer, outer)
    b = lax.broadcasted_iota(jnp.int32, (inner, kept), 0)
    kb = lax.broadcasted_iota(jnp.int32, (inner, kept), 1)
    cos_b, sin_b = cos_sin(b * kb % columns, columns)
    steps = kept // outer
    k1 = lax.broadcasted_iota(jnp.int32, (steps, columns), 0)
    x1 = lax.broadcasted_iota(jnp.int32, (steps, columns), 1)
    cos_u, sin_u = cos_sin(k1 * x1 % (columns // outer), columns // outer)
    k2 = lax.broadcasted_iota(jnp.int32, (outer, columns), 0)
    x2 = lax.broadcasted_iota(jnp.int32, (outer, columns), 1)
    cos_v, sin_v = cos_sin(k2 * x2 % columns, columns)
    return (cos_a, sin_a, cos_b, sin_b, cos_u, sin_u, cos_v, sin_v)


def row_tables(factors):
    cos_a, sin_a, cos_b, sin_b = factors[:4]
    columns = cos_a.shape[0] * cos_b.shape[0]
    kept = cos_a.shape[1]
    cos_t = cos_a[:, None, :] * cos_b[None, :, :] - sin_a[:, None, :] * sin_b[None, :, :]
    sin_t = sin_a[:, None, :] * cos_b[None, :, :] + cos_a[:, None, :] * sin_b[None, :, :]
    table = jnp.concatenate([cos_t, -sin_t], axis=2).reshape(columns, 2 * kept)
    return split_bf16(table)


def inverse_row_tables(factors):
    cos_u, sin_u, cos_v, sin_v = factors[4:]
    steps, columns = cos_u.shape
    outer = cos_v.shape[0]
    cos_t = cos_u[:, None, :] * cos_v[None, :, :] - sin_u[:, None, :] * sin_v[None, :, :]
    sin_t = sin_u[:, None, :] * cos_v[None, :, :] + cos_u[:, None, :] * sin_v[None, :, :]
    table = jnp.concatenate(
        [cos_t.reshape(steps * outer, columns), -sin_t.reshape(steps * outer, columns)], axis=0
    )
    return split_bf16(table)


def two_pass(eq, left, right_pair):
    return sum(
        jnp.einsum(eq, left, part, preferred_element_type=jnp.float32) for part in right_pair
    )


def column_tables(height):
    m = lax.broadcasted_iota(jnp.int32, (height, height), 0)
    y = lax.broadcasted_iota(jnp.int32, (height, height), 1)
    return cos_sin(m * y % height, height)


def block_complex(cos_t, sin_t, sign):
    return jnp.concatenate(
        [
            jnp.concatenate([cos_t, -sign * sin_t], axis=1),
            jnp.concatenate([sign * sin_t, cos_t], axis=1),
        ],
        axis=0,
    )


def score_fold(query_unit, targets, key_number):

    def add_block(carried, shard_piece, offset):
        scores = (
            jnp.einsum("qd,kd->qk", query_unit, shard_piece, preferred_element_type=jnp.float32)
            * score_scale
        )
        numbers = key_number(lax.broadcasted_iota(jnp.int32, (1, shard_piece.shape[0]), 1))
        exp_sums = jnp.sum(jnp.exp(scores), axis=1)
        picked = jnp.sum(jnp.where(targets[:, None] == numbers, scores, 0.0), axis=1)
        return (exp_sums, picked)

    return add_block


def same_number(gathered):
    return gathered


def body(
    pixels,
    depth_weight,
    mix_weight,
    spectral_real,
    spectral_imag,
    query_weight,
    key_weight,
    query_pixels,
    key_pixels,
    positives,
):
    slab_rows, groups, columns = pixels.shape
    half_cols = columns // 2
    channel = lax.axis_index("ch")
    group_count = lax.axis_size("ch")
    padded = extended(pixels, (("rows", 0),), DILATION)
    padded = jnp.pad(padded, ((0, 0), (0, 0), (DILATION, DILATION)))
    summed = pixels.astype(jnp.float32)
    for tap_row in range(3):
        for tap_col in range(3):
            shifted = padded[
                tap_row * DILATION : tap_row * DILATION + slab_rows,
                :,
                tap_col * DILATION : tap_col * DILATION + columns,
            ]
            summed = summed + depth_weight[:, 3 * tap_row + tap_col][
                None, :, None
            ] * shifted.astype(jnp.float32)
    conv_out = summed.astype(jnp.bfloat16)
    conv_out, factors = lax.optimization_barrier((conv_out, row_factors(columns, half_cols)))
    local_columns = lax.dynamic_slice_in_dim(mix_weight, channel * groups, groups, 1)
    ordered_rows = jnp.concatenate(
        [
            lax.dynamic_slice_in_dim(
                local_columns, (channel - shift) % group_count * groups, groups, 0
            )
            for shift in range(group_count)
        ],
        axis=0,
    )
    mixture = jnp.einsum(
        "rcw,cd->rdw",
        jnp.concatenate(ring_pieces(conv_out, "ch"), axis=1),
        ordered_rows,
        preferred_element_type=jnp.float32,
    )
    hidden = jax.nn.gelu(mixture).astype(jnp.bfloat16)
    table_pair = row_tables(factors)
    slabs = lax.axis_size("rows")
    spectrum = two_pass("rcx,xk->rck", hidden, table_pair)
    width = half_cols // slabs
    wire = spectrum.reshape(slab_rows, groups, 2, slabs, width)
    wire = jnp.transpose(wire, (2, 3, 0, 1, 4)).reshape(2, slabs, slab_rows, groups * width)
    columns_both = lax.all_to_all(
        wire.astype(jnp.bfloat16), "rows", split_axis=1, concat_axis=1, tiled=True
    )
    lanes = groups * width
    height = slabs * slab_rows
    column_cos, column_sin = column_tables(height)
    forward_pair = split_bf16(block_complex(column_cos, column_sin, -1.0))
    full = sum(
        jnp.einsum("my,yn->mn", part, columns_both.reshape(2 * height, lanes),
                   preferred_element_type=jnp.float32)
        for part in forward_pair
    )
    full_real, full_imag = full[:height], full[height:]
    kernel_real = spectral_real.astype(jnp.float32).reshape(height, lanes)
    kernel_imag = spectral_imag.astype(jnp.float32).reshape(height, lanes)
    product = jnp.concatenate(
        [full_real * kernel_real - full_imag * kernel_imag,
         full_real * kernel_imag + full_imag * kernel_real],
        axis=0,
    )
    back = jnp.einsum(
        "ym,mn->yn", block_complex(column_cos, column_sin, 1.0), product,
        precision=exact, preferred_element_type=jnp.float32,
    )
    back = (back * (1.0 / height)).astype(jnp.bfloat16)
    rows_both = lax.all_to_all(
        back.reshape(2, slabs, slab_rows, lanes), "rows", split_axis=1, concat_axis=1, tiled=True
    ).reshape(2, slabs, slab_rows, groups, width)
    rows_both = jnp.transpose(rows_both, (2, 3, 0, 1, 4)).reshape(slab_rows, groups, columns)
    doubling = jnp.where(lax.broadcasted_iota(jnp.int32, (1, 1, columns), 2) % half_cols == 0, 1.0, 2.0)
    weighting = doubling * (1.0 / columns)
    row_both = lax.optimization_barrier(rows_both * weighting.astype(jnp.bfloat16))
    spatial = two_pass("rck,kx->rcx", row_both, inverse_row_tables(factors))
    encoded = (hidden.astype(jnp.float32) + spatial).astype(jnp.bfloat16)
    key_count = key_pixels.shape[0]
    query_count = query_pixels.shape[0]
    quarter = query_count // group_count
    slab = lax.axis_index("rows")
    weights_all = jnp.concatenate(
        ring_pieces(jnp.concatenate([key_weight, query_weight], axis=1), "ch"), axis=0
    )
    sampled = jnp.concatenate([key_pixels, query_pixels])
    features = encoded[sampled // columns, :, sampled % columns]
    features = jnp.concatenate(ring_pieces(features, "ch"), axis=1)
    key_dim = key_weight.shape[1]
    key_unit = unit_rows(
        jnp.dot(features[:key_count], weights_all[:, :key_dim], preferred_element_type=jnp.float32)
    ).astype(jnp.bfloat16)
    own_queries = lax.dynamic_slice_in_dim(features, key_count + channel * quarter, quarter, 0)
    query_unit = unit_rows(
        jnp.dot(own_queries, weights_all[:, key_dim:], preferred_element_type=jnp.float32)
    ).astype(jnp.bfloat16)
    targets = lax.dynamic_slice_in_dim(positives, channel * quarter, quarter, 0)
    coded = jnp.concatenate([targets // 128, targets % 128]).astype(jnp.bfloat16)
    coded = jnp.pad(coded, (0, key_dim - 2 * quarter))[None, :]
    packet = jnp.concatenate([query_unit, coded], axis=0)
    gathered = lax.all_to_all(
        jnp.broadcast_to(packet[None], (slabs,) + packet.shape),
        "rows",
        split_axis=0,
        concat_axis=0,
        tiled=True,
    )
    all_queries = gathered[:, :quarter, :].reshape(-1, key_dim)
    coded_all = gathered[:, quarter, :].astype(jnp.int32)
    all_targets = (coded_all[:, :quarter] * 128 + coded_all[:, quarter : 2 * quarter]).reshape(-1)
    scores = (
        jnp.einsum("qd,kd->qk", all_queries, key_unit, preferred_element_type=jnp.float32)
        * score_scale
    )
    numbers = slab * key_count + lax.broadcasted_iota(jnp.int32, (1, key_count), 1)
    exp_sums = jnp.sum(jnp.exp(scores), axis=1)
    picked = jnp.sum(jnp.where(all_targets[:, None] == numbers, scores, 0.0), axis=1)
    reduced = lax.all_to_all(
        jnp.stack([exp_sums, picked], axis=1).reshape(slabs, quarter, 2),
        "rows",
        split_axis=0,
        concat_axis=0,
        tiled=True,
    ).sum(axis=0)
    losses = jnp.log(reduced[:, 0]) - reduced[:, 1]
    return (encoded, losses)


def solution(mesh):
    placed = (
        P("rows", "ch", None),
        P("ch", None),
        P(),
        P(None, "ch", "rows"),
        P(None, "ch", "rows"),
        P("ch", None),
        P("ch", None),
        P("rows"),
        P("rows"),
        P("rows"),
    )
    return jax.shard_map(
        body,
        mesh=mesh,
        in_specs=placed,
        out_specs=(P("rows", "ch", None), P(("rows", "ch"))),
        check_vma=False,
    )
```

```python
import jax
import jax.numpy as jnp
from jax import lax
from jax.sharding import PartitionSpec as P

DILATION = 2


score_scale = 10.0
exact = lax.Precision.HIGHEST


def extended(cells, sides, width):
    for axis, dim in sides:
        count = lax.axis_size(axis)
        ends = count - 1
        head = lax.slice_in_dim(cells, 0, width, axis=dim)
        tail = lax.slice_in_dim(cells, cells.shape[dim] - width, cells.shape[dim], axis=dim)
        cells = jnp.concatenate(
            [
                lax.ppermute(tail, axis, [(i, (i + 1) % count) for i in range(ends)]),
                cells,
                lax.ppermute(head, axis, [((i + 1) % count, i) for i in range(ends)]),
            ],
            axis=dim,
        )
    return cells


def ring_pieces(values, axis):
    count = lax.axis_size(axis)
    pieces = [values]
    for shift in range(1, count):
        pieces.append(
            lax.ppermute(values, axis, [(i, (i + shift) % count) for i in range(count)])
        )
    return pieces


def unit_rows(values):
    return values * lax.rsqrt(jnp.sum(values * values, axis=1, keepdims=True) + 1e-06)


def cos_sin(turns, length):
    angles = turns.astype(jnp.float32) * (2.0 * jnp.pi / length)
    return (jnp.cos(angles), jnp.sin(angles))


def split_bf16(table):
    high = table.astype(jnp.bfloat16)
    low = (table - high.astype(jnp.float32)).astype(jnp.bfloat16)
    return (high, low)


def row_factors(columns, kept):
    outer = 32
    inner = columns // outer
    a = lax.broadcasted_iota(jnp.int32, (outer, kept), 0)
    k = lax.broadcasted_iota(jnp.int32, (outer, kept), 1)
    cos_a, sin_a = cos_sin(a * k % outer, outer)
    b = lax.broadcasted_iota(jnp.int32, (inner, kept), 0)
    kb = lax.broadcasted_iota(jnp.int32, (inner, kept), 1)
    cos_b, sin_b = cos_sin(b * kb % columns, columns)
    return (cos_a, sin_a, cos_b, sin_b)


def row_tables(factors):
    cos_a, sin_a, cos_b, sin_b = factors
    columns = cos_a.shape[0] * cos_b.shape[0]
    kept = cos_a.shape[1]
    cos_t = cos_a[:, None, :] * cos_b[None, :, :] - sin_a[:, None, :] * sin_b[None, :, :]
    sin_t = sin_a[:, None, :] * cos_b[None, :, :] + cos_a[:, None, :] * sin_b[None, :, :]
    table = jnp.concatenate([cos_t, -sin_t], axis=2).reshape(columns, 2 * kept)
    return split_bf16(table)


def two_pass(eq, left, right_pair):
    return sum(
        jnp.einsum(eq, left, part, preferred_element_type=jnp.float32) for part in right_pair
    )


def column_tables(height):
    m = lax.broadcasted_iota(jnp.int32, (height, height), 0)
    y = lax.broadcasted_iota(jnp.int32, (height, height), 1)
    return cos_sin(m * y % height, height)


def block_complex(cos_t, sin_t, sign):
    return jnp.concatenate(
        [
            jnp.concatenate([cos_t, -sign * sin_t], axis=1),
            jnp.concatenate([sign * sin_t, cos_t], axis=1),
        ],
        axis=0,
    )


def score_fold(query_unit, targets, key_number):

    def add_block(carried, shard_piece, offset):
        scores = (
            jnp.einsum("qd,kd->qk", query_unit, shard_piece, preferred_element_type=jnp.float32)
            * score_scale
        )
        numbers = key_number(lax.broadcasted_iota(jnp.int32, (1, shard_piece.shape[0]), 1))
        exp_sums = jnp.sum(jnp.exp(scores), axis=1)
        picked = jnp.sum(jnp.where(targets[:, None] == numbers, scores, 0.0), axis=1)
        return (exp_sums, picked)

    return add_block


def same_number(gathered):
    return gathered


def body(
    pixels,
    depth_weight,
    mix_weight,
    spectral_real,
    spectral_imag,
    query_weight,
    key_weight,
    query_pixels,
    key_pixels,
    positives,
):
    slab_rows, groups, columns = pixels.shape
    half_cols = columns // 2
    channel = lax.axis_index("ch")
    group_count = lax.axis_size("ch")
    padded = extended(pixels, (("rows", 0),), DILATION)
    padded = jnp.pad(padded, ((0, 0), (0, 0), (DILATION, DILATION)))
    summed = pixels.astype(jnp.float32)
    for tap_row in range(3):
        for tap_col in range(3):
            shifted = padded[
                tap_row * DILATION : tap_row * DILATION + slab_rows,
                :,
                tap_col * DILATION : tap_col * DILATION + columns,
            ]
            summed = summed + depth_weight[:, 3 * tap_row + tap_col][
                None, :, None
            ] * shifted.astype(jnp.float32)
    conv_out = summed.astype(jnp.bfloat16)
    conv_out, factors = lax.optimization_barrier((conv_out, row_factors(columns, half_cols)))
    local_columns = lax.dynamic_slice_in_dim(mix_weight, channel * groups, groups, 1)
    ordered_rows = jnp.concatenate(
        [
            lax.dynamic_slice_in_dim(
                local_columns, (channel - shift) % group_count * groups, groups, 0
            )
            for shift in range(group_count)
        ],
        axis=0,
    )
    mixture = jnp.einsum(
        "rcw,cd->rdw",
        jnp.concatenate(ring_pieces(conv_out, "ch"), axis=1),
        ordered_rows,
        preferred_element_type=jnp.float32,
    )
    hidden = jax.nn.gelu(mixture).astype(jnp.bfloat16)
    table_pair = row_tables(factors)
    slabs = lax.axis_size("rows")
    spectrum = two_pass("rcx,xk->rck", hidden, table_pair)
    width = half_cols // slabs
    wire = spectrum.reshape(slab_rows, groups, 2, slabs, width)
    wire = jnp.transpose(wire, (2, 3, 0, 1, 4)).reshape(2, slabs, slab_rows, groups * width)
    columns_both = lax.all_to_all(
        wire.astype(jnp.bfloat16), "rows", split_axis=1, concat_axis=1, tiled=True
    )
    lanes = groups * width
    height = slabs * slab_rows
    column_cos, column_sin = column_tables(height)
    forward_pair = split_bf16(block_complex(column_cos, column_sin, -1.0))
    full = sum(
        jnp.einsum("my,yn->mn", part, columns_both.reshape(2 * height, lanes),
                   preferred_element_type=jnp.float32)
        for part in forward_pair
    )
    full_real, full_imag = full[:height], full[height:]
    kernel_real = spectral_real.astype(jnp.float32).reshape(height, lanes)
    kernel_imag = spectral_imag.astype(jnp.float32).reshape(height, lanes)
    product = jnp.concatenate(
        [full_real * kernel_real - full_imag * kernel_imag,
         full_real * kernel_imag + full_imag * kernel_real],
        axis=0,
    )
    back = jnp.einsum(
        "ym,mn->yn", block_complex(column_cos, column_sin, 1.0), product,
        precision=exact, preferred_element_type=jnp.float32,
    )
    back = (back * (1.0 / height)).astype(jnp.bfloat16)
    rows_both = lax.all_to_all(
        back.reshape(2, slabs, slab_rows, lanes), "rows", split_axis=1, concat_axis=1, tiled=True
    ).reshape(2, slabs, slab_rows, groups, width)
    rows_both = jnp.transpose(rows_both, (2, 3, 0, 1, 4)).reshape(slab_rows, groups, columns)
    doubling = jnp.where(lax.broadcasted_iota(jnp.int32, (1, 1, columns), 2) % half_cols == 0, 1.0, 2.0)
    weighting = doubling * (1.0 / columns)
    row_both = lax.optimization_barrier(rows_both * weighting.astype(jnp.bfloat16))
    parity = lax.broadcasted_iota(jnp.int32, (1, 1, columns), 2) % 2
    signs = jnp.where(parity == 0, 1.0, -1.0).astype(jnp.bfloat16)
    both_halves = jnp.concatenate([row_both, row_both * signs], axis=0)
    halves = two_pass("rck,xk->rcx", both_halves, tuple(part[:half_cols] for part in table_pair))
    spatial = jnp.concatenate([halves[:slab_rows], halves[slab_rows:]], axis=2)
    encoded = (hidden.astype(jnp.float32) + spatial).astype(jnp.bfloat16)
    key_count = key_pixels.shape[0]
    query_count = query_pixels.shape[0]
    quarter = query_count // group_count
    slab = lax.axis_index("rows")
    weights_all = jnp.concatenate(
        ring_pieces(jnp.concatenate([key_weight, query_weight], axis=1), "ch"), axis=0
    )
    sampled = jnp.concatenate([key_pixels, query_pixels])
    features = encoded[sampled // columns, :, sampled % columns]
    features = jnp.concatenate(ring_pieces(features, "ch"), axis=1)
    key_dim = key_weight.shape[1]
    key_unit = unit_rows(
        jnp.dot(features[:key_count], weights_all[:, :key_dim], preferred_element_type=jnp.float32)
    ).astype(jnp.bfloat16)
    own_queries = lax.dynamic_slice_in_dim(features, key_count + channel * quarter, quarter, 0)
    query_unit = unit_rows(
        jnp.dot(own_queries, weights_all[:, key_dim:], preferred_element_type=jnp.float32)
    ).astype(jnp.bfloat16)
    targets = lax.dynamic_slice_in_dim(positives, channel * quarter, quarter, 0)
    coded = jnp.concatenate([targets // 128, targets % 128]).astype(jnp.bfloat16)
    coded = jnp.pad(coded, (0, key_dim - 2 * quarter))[None, :]
    packet = jnp.concatenate([query_unit, coded], axis=0)
    gathered = lax.all_to_all(
        jnp.broadcast_to(packet[None], (slabs,) + packet.shape),
        "rows",
        split_axis=0,
        concat_axis=0,
        tiled=True,
    )
    all_queries = gathered[:, :quarter, :].reshape(-1, key_dim)
    coded_all = gathered[:, quarter, :].astype(jnp.int32)
    all_targets = (coded_all[:, :quarter] * 128 + coded_all[:, quarter : 2 * quarter]).reshape(-1)
    scores = (
        jnp.einsum("qd,kd->qk", all_queries, key_unit, preferred_element_type=jnp.float32)
        * score_scale
    )
    numbers = slab * key_count + lax.broadcasted_iota(jnp.int32, (1, key_count), 1)
    exp_sums = jnp.sum(jnp.exp(scores), axis=1)
    picked = jnp.sum(jnp.where(all_targets[:, None] == numbers, scores, 0.0), axis=1)
    reduced = lax.all_to_all(
        jnp.stack([exp_sums, picked], axis=1).reshape(slabs, quarter, 2),
        "rows",
        split_axis=0,
        concat_axis=0,
        tiled=True,
    ).sum(axis=0)
    losses = jnp.log(reduced[:, 0]) - reduced[:, 1]
    return (encoded, losses)


def solution(mesh):
    placed = (
        P("rows", "ch", None),
        P("ch", None),
        P(),
        P(None, "ch", "rows"),
        P(None, "ch", "rows"),
        P("ch", None),
        P("ch", None),
        P("rows"),
        P("rows"),
        P("rows"),
    )
    return jax.shard_map(
        body,
        mesh=mesh,
        in_specs=placed,
        out_specs=(P("rows", "ch", None), P(("rows", "ch"))),
        check_vma=False,
    )
```

```python
import jax
import jax.numpy as jnp
from jax import lax
from jax.sharding import PartitionSpec as P

DILATION = 2


score_scale = 10.0
exact = lax.Precision.HIGHEST


def extended(cells, sides, width):
    for axis, dim in sides:
        count = lax.axis_size(axis)
        ends = count - 1
        head = lax.slice_in_dim(cells, 0, width, axis=dim)
        tail = lax.slice_in_dim(cells, cells.shape[dim] - width, cells.shape[dim], axis=dim)
        cells = jnp.concatenate(
            [
                lax.ppermute(tail, axis, [(i, (i + 1) % count) for i in range(ends)]),
                cells,
                lax.ppermute(head, axis, [((i + 1) % count, i) for i in range(ends)]),
            ],
            axis=dim,
        )
    return cells


def ring_pieces(values, axis):
    count = lax.axis_size(axis)
    pieces = [values]
    for shift in range(1, count):
        pieces.append(
            lax.ppermute(values, axis, [(i, (i + shift) % count) for i in range(count)])
        )
    return pieces


def unit_rows(values):
    return values * lax.rsqrt(jnp.sum(values * values, axis=1, keepdims=True) + 1e-06)


def cos_sin(turns, length):
    angles = turns.astype(jnp.float32) * (2.0 * jnp.pi / length)
    return (jnp.cos(angles), jnp.sin(angles))


def split_bf16(table):
    high = table.astype(jnp.bfloat16)
    low = (table - high.astype(jnp.float32)).astype(jnp.bfloat16)
    return (high, low)


def row_factors(columns, kept):
    outer = 32
    inner = columns // outer
    a = lax.broadcasted_iota(jnp.int32, (outer, kept), 0)
    k = lax.broadcasted_iota(jnp.int32, (outer, kept), 1)
    cos_a, sin_a = cos_sin(a * k % outer, outer)
    b = lax.broadcasted_iota(jnp.int32, (inner, kept), 0)
    kb = lax.broadcasted_iota(jnp.int32, (inner, kept), 1)
    cos_b, sin_b = cos_sin(b * kb % columns, columns)
    return (cos_a, sin_a, cos_b, sin_b)


def row_tables(factors):
    cos_a, sin_a, cos_b, sin_b = factors
    columns = cos_a.shape[0] * cos_b.shape[0]
    kept = cos_a.shape[1]
    cos_t = cos_a[:, None, :] * cos_b[None, :, :] - sin_a[:, None, :] * sin_b[None, :, :]
    sin_t = sin_a[:, None, :] * cos_b[None, :, :] + cos_a[:, None, :] * sin_b[None, :, :]
    table = jnp.concatenate([cos_t, -sin_t], axis=2).reshape(columns, 2 * kept)
    return split_bf16(table)


def two_pass(eq, left, right_pair):
    return sum(
        jnp.einsum(eq, left, part, preferred_element_type=jnp.float32) for part in right_pair
    )


def column_tables(height):
    m = lax.broadcasted_iota(jnp.int32, (height, height), 0)
    y = lax.broadcasted_iota(jnp.int32, (height, height), 1)
    return cos_sin(m * y % height, height)


def block_complex(cos_t, sin_t, sign):
    return jnp.concatenate(
        [
            jnp.concatenate([cos_t, -sign * sin_t], axis=1),
            jnp.concatenate([sign * sin_t, cos_t], axis=1),
        ],
        axis=0,
    )


def score_fold(query_unit, targets, key_number):

    def add_block(carried, shard_piece, offset):
        scores = (
            jnp.einsum("qd,kd->qk", query_unit, shard_piece, preferred_element_type=jnp.float32)
            * score_scale
        )
        numbers = key_number(lax.broadcasted_iota(jnp.int32, (1, shard_piece.shape[0]), 1))
        exp_sums = jnp.sum(jnp.exp(scores), axis=1)
        picked = jnp.sum(jnp.where(targets[:, None] == numbers, scores, 0.0), axis=1)
        return (exp_sums, picked)

    return add_block


def same_number(gathered):
    return gathered


def body(
    pixels,
    depth_weight,
    mix_weight,
    spectral_real,
    spectral_imag,
    query_weight,
    key_weight,
    query_pixels,
    key_pixels,
    positives,
):
    slab_rows, groups, columns = pixels.shape
    half_cols = columns // 2
    channel = lax.axis_index("ch")
    group_count = lax.axis_size("ch")
    padded = extended(pixels, (("rows", 0),), DILATION)
    padded = jnp.pad(padded, ((0, 0), (0, 0), (DILATION, DILATION)))
    summed = pixels.astype(jnp.float32)
    for tap_row in range(3):
        for tap_col in range(3):
            shifted = padded[
                tap_row * DILATION : tap_row * DILATION + slab_rows,
                :,
                tap_col * DILATION : tap_col * DILATION + columns,
            ]
            summed = summed + depth_weight[:, 3 * tap_row + tap_col][
                None, :, None
            ] * shifted.astype(jnp.float32)
    conv_out = summed.astype(jnp.bfloat16)
    conv_out, factors = lax.optimization_barrier((conv_out, row_factors(columns, half_cols)))
    local_columns = lax.dynamic_slice_in_dim(mix_weight, channel * groups, groups, 1)
    ordered_rows = jnp.concatenate(
        [
            lax.dynamic_slice_in_dim(
                local_columns, (channel - shift) % group_count * groups, groups, 0
            )
            for shift in range(group_count)
        ],
        axis=0,
    )
    mixture = jnp.einsum(
        "rcw,cd->rdw",
        jnp.concatenate(ring_pieces(conv_out, "ch"), axis=1),
        ordered_rows,
        preferred_element_type=jnp.float32,
    )
    hidden = jax.nn.gelu(mixture).astype(jnp.bfloat16)
    table_pair = row_tables(factors)
    slabs = lax.axis_size("rows")
    spectrum = two_pass("rcx,xk->rck", hidden, table_pair)
    width = half_cols // slabs
    wire = spectrum.reshape(slab_rows, groups, 2, slabs, width)
    wire = jnp.transpose(wire, (2, 3, 0, 1, 4)).reshape(2, slabs, slab_rows, groups * width)
    columns_both = lax.all_to_all(
        wire.astype(jnp.bfloat16), "rows", split_axis=1, concat_axis=1, tiled=True
    )
    lanes = groups * width
    height = slabs * slab_rows
    column_cos, column_sin = column_tables(height)
    forward_pair = split_bf16(block_complex(column_cos, column_sin, -1.0))
    full = sum(
        jnp.einsum("my,yn->mn", part, columns_both.reshape(2 * height, lanes),
                   preferred_element_type=jnp.float32)
        for part in forward_pair
    )
    full_real, full_imag = full[:height], full[height:]
    kernel_real = spectral_real.astype(jnp.float32).reshape(height, lanes)
    kernel_imag = spectral_imag.astype(jnp.float32).reshape(height, lanes)
    product = jnp.concatenate(
        [full_real * kernel_real - full_imag * kernel_imag,
         full_real * kernel_imag + full_imag * kernel_real],
        axis=0,
    )
    back = jnp.einsum(
        "ym,mn->yn", block_complex(column_cos, column_sin, 1.0), product,
        precision=exact, preferred_element_type=jnp.float32,
    )
    back = (back * (1.0 / height)).astype(jnp.bfloat16)
    rows_both = lax.all_to_all(
        back.reshape(2, slabs, slab_rows, lanes), "rows", split_axis=1, concat_axis=1, tiled=True
    ).reshape(2, slabs, slab_rows, groups, width)
    rows_both = jnp.transpose(rows_both, (2, 3, 0, 1, 4)).reshape(slab_rows, groups, columns)
    doubling = jnp.where(lax.broadcasted_iota(jnp.int32, (1, 1, columns), 2) % half_cols == 0, 1.0, 2.0)
    weighting = doubling * (1.0 / columns)
    row_both = lax.optimization_barrier(rows_both * weighting.astype(jnp.bfloat16))
    spatial = two_pass("rck,xk->rcx", row_both, table_pair)
    encoded = (hidden.astype(jnp.float32) + spatial).astype(jnp.bfloat16)
    key_count = key_pixels.shape[0]
    query_count = query_pixels.shape[0]
    quarter = query_count // group_count
    slab = lax.axis_index("rows")
    weights_all = jnp.concatenate(
        ring_pieces(jnp.concatenate([key_weight, query_weight], axis=1), "ch"), axis=0
    )
    sampled = jnp.concatenate([key_pixels, query_pixels])
    places = lax.broadcasted_iota(jnp.int32, (1, slab_rows, columns), 1) * columns
    places = places + lax.broadcasted_iota(jnp.int32, (1, slab_rows, columns), 2)
    chosen = (sampled[:, None, None] == places).astype(jnp.bfloat16)
    features = jnp.einsum(
        "npx,pcx->nc", chosen, encoded, preferred_element_type=jnp.float32
    ).astype(jnp.bfloat16)
    features = jnp.concatenate(ring_pieces(features, "ch"), axis=1)
    key_dim = key_weight.shape[1]
    key_unit = unit_rows(
        jnp.dot(features[:key_count], weights_all[:, :key_dim], preferred_element_type=jnp.float32)
    ).astype(jnp.bfloat16)
    own_queries = lax.dynamic_slice_in_dim(features, key_count + channel * quarter, quarter, 0)
    query_unit = unit_rows(
        jnp.dot(own_queries, weights_all[:, key_dim:], preferred_element_type=jnp.float32)
    ).astype(jnp.bfloat16)
    targets = lax.dynamic_slice_in_dim(positives, channel * quarter, quarter, 0)
    coded = jnp.concatenate([targets // 128, targets % 128]).astype(jnp.bfloat16)
    coded = jnp.pad(coded, (0, key_dim - 2 * quarter))[None, :]
    packet = jnp.concatenate([query_unit, coded], axis=0)
    gathered = lax.all_to_all(
        jnp.broadcast_to(packet[None], (slabs,) + packet.shape),
        "rows",
        split_axis=0,
        concat_axis=0,
        tiled=True,
    )
    all_queries = gathered[:, :quarter, :].reshape(-1, key_dim)
    coded_all = gathered[:, quarter, :].astype(jnp.int32)
    all_targets = (coded_all[:, :quarter] * 128 + coded_all[:, quarter : 2 * quarter]).reshape(-1)
    scores = (
        jnp.einsum("qd,kd->qk", all_queries, key_unit, preferred_element_type=jnp.float32)
        * score_scale
    )
    numbers = slab * key_count + lax.broadcasted_iota(jnp.int32, (1, key_count), 1)
    exp_sums = jnp.sum(jnp.exp(scores), axis=1)
    picked = jnp.sum(jnp.where(all_targets[:, None] == numbers, scores, 0.0), axis=1)
    reduced = lax.all_to_all(
        jnp.stack([exp_sums, picked], axis=1).reshape(slabs, quarter, 2),
        "rows",
        split_axis=0,
        concat_axis=0,
        tiled=True,
    ).sum(axis=0)
    losses = jnp.log(reduced[:, 0]) - reduced[:, 1]
    return (encoded, losses)


def solution(mesh):
    placed = (
        P("rows", "ch", None),
        P("ch", None),
        P(),
        P(None, "ch", "rows"),
        P(None, "ch", "rows"),
        P("ch", None),
        P("ch", None),
        P("rows"),
        P("rows"),
        P("rows"),
    )
    return jax.shard_map(
        body,
        mesh=mesh,
        in_specs=placed,
        out_specs=(P("rows", "ch", None), P(("rows", "ch"))),
        check_vma=False,
    )
```

```python
import jax
import jax.numpy as jnp
from jax import lax
from jax.sharding import PartitionSpec as P

DILATION = 2


score_scale = 10.0
exact = lax.Precision.HIGHEST


def extended(cells, sides, width):
    for axis, dim in sides:
        count = lax.axis_size(axis)
        ends = count - 1
        head = lax.slice_in_dim(cells, 0, width, axis=dim)
        tail = lax.slice_in_dim(cells, cells.shape[dim] - width, cells.shape[dim], axis=dim)
        cells = jnp.concatenate(
            [
                lax.ppermute(tail, axis, [(i, (i + 1) % count) for i in range(ends)]),
                cells,
                lax.ppermute(head, axis, [((i + 1) % count, i) for i in range(ends)]),
            ],
            axis=dim,
        )
    return cells


def ring_pieces(values, axis):
    count = lax.axis_size(axis)
    pieces = [values]
    for shift in range(1, count):
        pieces.append(
            lax.ppermute(values, axis, [(i, (i + shift) % count) for i in range(count)])
        )
    return pieces


def unit_rows(values):
    return values * lax.rsqrt(jnp.sum(values * values, axis=1, keepdims=True) + 1e-06)


def cos_sin(turns, length):
    angles = turns.astype(jnp.float32) * (2.0 * jnp.pi / length)
    return (jnp.cos(angles), jnp.sin(angles))


def split_bf16(table):
    high = table.astype(jnp.bfloat16)
    low = (table - high.astype(jnp.float32)).astype(jnp.bfloat16)
    return (high, low)


def row_factors(columns, kept):
    outer = 32
    inner = columns // outer
    a = lax.broadcasted_iota(jnp.int32, (outer, kept), 0)
    k = lax.broadcasted_iota(jnp.int32, (outer, kept), 1)
    cos_a, sin_a = cos_sin(a * k % outer, outer)
    b = lax.broadcasted_iota(jnp.int32, (inner, kept), 0)
    kb = lax.broadcasted_iota(jnp.int32, (inner, kept), 1)
    cos_b, sin_b = cos_sin(b * kb % columns, columns)
    return (cos_a, sin_a, cos_b, sin_b)


def row_tables(factors):
    cos_a, sin_a, cos_b, sin_b = factors
    columns = cos_a.shape[0] * cos_b.shape[0]
    kept = cos_a.shape[1]
    cos_t = cos_a[:, None, :] * cos_b[None, :, :] - sin_a[:, None, :] * sin_b[None, :, :]
    sin_t = sin_a[:, None, :] * cos_b[None, :, :] + cos_a[:, None, :] * sin_b[None, :, :]
    table = jnp.concatenate([cos_t, -sin_t], axis=2).reshape(columns, 2 * kept)
    return split_bf16(table)


def two_pass(eq, left, right_pair):
    return sum(
        jnp.einsum(eq, left, part, preferred_element_type=jnp.float32) for part in right_pair
    )


def column_tables(height):
    m = lax.broadcasted_iota(jnp.int32, (height, height), 0)
    y = lax.broadcasted_iota(jnp.int32, (height, height), 1)
    return cos_sin(m * y % height, height)


def block_complex(cos_t, sin_t, sign):
    return jnp.concatenate(
        [
            jnp.concatenate([cos_t, -sign * sin_t], axis=1),
            jnp.concatenate([sign * sin_t, cos_t], axis=1),
        ],
        axis=0,
    )


def score_fold(query_unit, targets, key_number):

    def add_block(carried, shard_piece, offset):
        scores = (
            jnp.einsum("qd,kd->qk", query_unit, shard_piece, preferred_element_type=jnp.float32)
            * score_scale
        )
        numbers = key_number(lax.broadcasted_iota(jnp.int32, (1, shard_piece.shape[0]), 1))
        exp_sums = jnp.sum(jnp.exp(scores), axis=1)
        picked = jnp.sum(jnp.where(targets[:, None] == numbers, scores, 0.0), axis=1)
        return (exp_sums, picked)

    return add_block


def same_number(gathered):
    return gathered


def body(
    pixels,
    depth_weight,
    mix_weight,
    spectral_real,
    spectral_imag,
    query_weight,
    key_weight,
    query_pixels,
    key_pixels,
    positives,
):
    slab_rows, groups, columns = pixels.shape
    half_cols = columns // 2
    channel = lax.axis_index("ch")
    group_count = lax.axis_size("ch")
    padded = extended(pixels, (("rows", 0),), DILATION)
    padded = jnp.pad(padded, ((0, 0), (0, 0), (DILATION, DILATION)))
    summed = pixels.astype(jnp.float32)
    for tap_row in range(3):
        for tap_col in range(3):
            shifted = padded[
                tap_row * DILATION : tap_row * DILATION + slab_rows,
                :,
                tap_col * DILATION : tap_col * DILATION + columns,
            ]
            summed = summed + depth_weight[:, 3 * tap_row + tap_col][
                None, :, None
            ] * shifted.astype(jnp.float32)
    conv_out = summed.astype(jnp.bfloat16)
    conv_out, factors = lax.optimization_barrier((conv_out, row_factors(columns, half_cols)))
    local_columns = lax.dynamic_slice_in_dim(mix_weight, channel * groups, groups, 1)
    ordered_rows = jnp.concatenate(
        [
            lax.dynamic_slice_in_dim(
                local_columns, (channel - shift) % group_count * groups, groups, 0
            )
            for shift in range(group_count)
        ],
        axis=0,
    )
    mixture = jnp.einsum(
        "rcw,cd->rdw",
        jnp.concatenate(ring_pieces(conv_out, "ch"), axis=1),
        ordered_rows,
        preferred_element_type=jnp.float32,
    )
    hidden = jax.nn.gelu(mixture).astype(jnp.bfloat16)
    table_pair = row_tables(factors)
    slabs = lax.axis_size("rows")
    spectrum = two_pass("rcx,xk->rck", hidden, table_pair)
    width = half_cols // slabs
    wire = spectrum.reshape(slab_rows, groups, 2, slabs, width)
    wire = jnp.transpose(wire, (2, 3, 0, 1, 4)).reshape(2, slabs, slab_rows, groups * width)
    columns_both = lax.all_to_all(
        wire.astype(jnp.bfloat16), "rows", split_axis=1, concat_axis=1, tiled=True
    )
    lanes = groups * width
    height = slabs * slab_rows
    column_cos, column_sin = column_tables(height)
    forward_pair = split_bf16(block_complex(column_cos, column_sin, -1.0))
    full = sum(
        jnp.einsum("my,yn->mn", part, columns_both.reshape(2 * height, lanes),
                   preferred_element_type=jnp.float32)
        for part in forward_pair
    )
    full_real, full_imag = full[:height], full[height:]
    kernel_real = spectral_real.astype(jnp.float32).reshape(height, lanes)
    kernel_imag = spectral_imag.astype(jnp.float32).reshape(height, lanes)
    product = jnp.concatenate(
        [full_real * kernel_real - full_imag * kernel_imag,
         full_real * kernel_imag + full_imag * kernel_real],
        axis=0,
    )
    back = jnp.einsum(
        "ym,mn->yn", block_complex(column_cos, column_sin, 1.0), product,
        precision=exact, preferred_element_type=jnp.float32,
    )
    back = (back * (1.0 / height)).astype(jnp.bfloat16)
    rows_both = lax.all_to_all(
        back.reshape(2, slabs, slab_rows, lanes), "rows", split_axis=1, concat_axis=1, tiled=True
    ).reshape(2, slabs, slab_rows, groups, width)
    rows_both = jnp.transpose(rows_both, (2, 3, 0, 1, 4)).reshape(slab_rows, groups, columns)
    doubling = jnp.where(lax.broadcasted_iota(jnp.int32, (1, 1, columns), 2) % half_cols == 0, 1.0, 2.0)
    weighting = doubling * (1.0 / columns)
    row_both = lax.optimization_barrier(rows_both * weighting.astype(jnp.bfloat16))
    spatial = two_pass("rck,xk->rcx", row_both, table_pair)
    encoded = (hidden.astype(jnp.float32) + spatial).astype(jnp.bfloat16)
    key_count = key_pixels.shape[0]
    query_count = query_pixels.shape[0]
    quarter = query_count // group_count
    slab = lax.axis_index("rows")
    weights_all = jnp.concatenate(
        ring_pieces(jnp.concatenate([key_weight, query_weight], axis=1), "ch"), axis=0
    )
    sampled = jnp.concatenate([key_pixels, query_pixels])
    places = lax.broadcasted_iota(jnp.int32, (1, slab_rows, columns), 1) * columns
    places = places + lax.broadcasted_iota(jnp.int32, (1, slab_rows, columns), 2)
    chosen = (sampled[:, None, None] == places).astype(jnp.bfloat16)
    features = jnp.einsum(
        "npx,pcx->nc", chosen, encoded, preferred_element_type=jnp.float32
    ).astype(jnp.bfloat16)
    features = jnp.concatenate(ring_pieces(features, "ch"), axis=1)
    key_dim = key_weight.shape[1]
    key_unit = unit_rows(
        jnp.dot(features[:key_count], weights_all[:, :key_dim], preferred_element_type=jnp.float32)
    ).astype(jnp.bfloat16)
    own_queries = lax.dynamic_slice_in_dim(features, key_count + channel * quarter, quarter, 0)
    query_unit = unit_rows(
        jnp.dot(own_queries, weights_all[:, key_dim:], preferred_element_type=jnp.float32)
    ).astype(jnp.bfloat16)
    targets = lax.dynamic_slice_in_dim(positives, channel * quarter, quarter, 0)
    gathered = lax.all_to_all(
        jnp.broadcast_to(query_unit[None], (slabs,) + query_unit.shape),
        "rows",
        split_axis=0,
        concat_axis=0,
        tiled=True,
    )
    all_queries = gathered.reshape(-1, key_dim)
    all_targets = lax.all_to_all(
        jnp.broadcast_to(targets[None], (slabs, quarter)),
        "rows",
        split_axis=0,
        concat_axis=0,
        tiled=True,
    ).reshape(-1)
    scores = (
        jnp.einsum("qd,kd->qk", all_queries, key_unit, preferred_element_type=jnp.float32)
        * score_scale
    )
    numbers = slab * key_count + lax.broadcasted_iota(jnp.int32, (1, key_count), 1)
    exp_sums = jnp.sum(jnp.exp(scores), axis=1)
    picked = jnp.sum(jnp.where(all_targets[:, None] == numbers, scores, 0.0), axis=1)
    reduced = lax.all_to_all(
        jnp.stack([exp_sums, picked], axis=1).reshape(slabs, quarter, 2),
        "rows",
        split_axis=0,
        concat_axis=0,
        tiled=True,
    ).sum(axis=0)
    losses = jnp.log(reduced[:, 0]) - reduced[:, 1]
    return (encoded, losses)


def solution(mesh):
    placed = (
        P("rows", "ch", None),
        P("ch", None),
        P(),
        P(None, "ch", "rows"),
        P(None, "ch", "rows"),
        P("ch", None),
        P("ch", None),
        P("rows"),
        P("rows"),
        P("rows"),
    )
    return jax.shard_map(
        body,
        mesh=mesh,
        in_specs=placed,
        out_specs=(P("rows", "ch", None), P(("rows", "ch"))),
        check_vma=False,
    )
```
